256 devices in a mesh: chan: 8 (over x, core), filt: 32 (over y, z).
Axes of the slice: x: 4, y: 4, z: 8, core: 2. Of those that a mesh axis runs over, the one named last changes fastest.
Arguments:
- inputs: bfloat16 [1, 64, 128, 1024], P(None, 'filt', None, 'chan'), may hold values from -6 to 6
- weights: bfloat16 [3, 3, 1024, 1024], P(None, None, 'filt', 'chan'), may hold values from -0.0625 to 0.0625
- cotangent: bfloat16 [1, 64, 1024, 128], P(None, 'chan', 'filt'), may hold values from -6 to 6
Outputs:
- outputs: bfloat16 [1, 64, 1024, 128], P(None, 'chan', 'filt')
- input_grad: bfloat16 [1, 64, 128, 1024], P(None, 'filt', None, 'chan')
- weight_grad: float32 [3, 3, 1024, 1024], P(None, None, 'filt', 'chan')
The draws below stay inside these ranges and needn't reach their ends.
All inputs are finite; a program needn't handle non-finite values.
Results may differ from the reference program's by a relative error of at most 0.001.
Values may be sent and summed in bfloat16 or wider, within the bound.
A program may use at most 128 MiB of HBM per device.

```python
import math
import jax
import jax.numpy as jnp

CIN = 1024
COUT = 1024
BATCH = 1
HEIGHT = 64
WIDTH = 128


def block_scale(rng, dims, pieces, smallest, high):
    loudness = 1.0
    for dim, blocks in pieces:
        steps = jax.random.uniform(jax.random.fold_in(jax.random.fold_in(rng, 6), dim), (blocks,), jnp.float32, smallest / len(pieces), high / len(pieces))
        loudness = loudness * jnp.repeat(jnp.exp(steps), dims[dim] // blocks).reshape((-1,) + (1,) * (len(dims) - 1 - dim))
    return loudness


def gaussian(stream_key, shape, scale, reach, cuts=(), dtype=jnp.bfloat16):
    values = jax.random.normal(stream_key, shape, jnp.float32) * scale
    if len(cuts) > 0:
        values = block_scale(stream_key, shape, cuts, -0.22, 0.18) * values
    return jnp.clip(values, min=-reach, max=reach).astype(dtype)


def setup_inputs(seed: int = 0) -> dict:
    key_of = jax.random.split(jax.random.key(seed), 4)
    return {
        "inputs": gaussian(key_of[0], (BATCH, HEIGHT, WIDTH, CIN), 1.0, 6.0, ((1, 32), (3, 8))),
        "weights": gaussian(key_of[1], (3, 3, COUT, CIN), (9 * CIN) ** -0.5, 0.0625, ((2, 32), (3, 8))),
        "cotangent": gaussian(key_of[2], (BATCH, HEIGHT, COUT, WIDTH), 1.0, 6.0, ((1, 8), (2, 32))),
    }


def window(padded, tap_row, tap_col):
    return padded[:, tap_row:tap_row + HEIGHT, tap_col:tap_col + WIDTH, :].reshape(-1, padded.shape[3])

def reference(inputs, weights, cotangent):
    cot_last = jnp.transpose(cotangent, (0, 1, 3, 2))
    padded_in = jnp.pad(inputs, ((0, 0), (1, 1), (1, 1), (0, 0))).astype(jnp.float32)
    padded_cot = jnp.pad(cot_last, ((0, 0), (1, 1), (1, 1), (0, 0))).astype(jnp.float32)
    kernel = weights.astype(jnp.float32)
    cot_flat = cot_last.astype(jnp.float32).reshape(-1, COUT)
    summed_out = jnp.zeros((BATCH * HEIGHT * WIDTH, COUT), jnp.float32)
    summed_grad = jnp.zeros((BATCH * HEIGHT * WIDTH, CIN), jnp.float32)
    grad_taps = []
    norm_factor = 1.0 / math.sqrt(BATCH * HEIGHT * WIDTH)
    for tap_row in range(3):
        for tap_col in range(3):
            source = window(padded_in, tap_row, tap_col)
            summed_out = summed_out + jnp.dot(source, kernel[tap_row, tap_col].T, preferred_element_type=jnp.float32)
            back = window(padded_cot, 2 - tap_row, 2 - tap_col)
            summed_grad = summed_grad + jnp.dot(back, kernel[tap_row, tap_col], preferred_element_type=jnp.float32)
            grad_taps.append(jnp.dot(cot_flat.T, source, preferred_element_type=jnp.float32) * norm_factor)
    outputs = jnp.transpose(summed_out.reshape(BATCH, HEIGHT, WIDTH, COUT), (0, 1, 3, 2)).astype(jnp.bfloat16)
    input_grad = summed_grad.reshape(BATCH, HEIGHT, WIDTH, CIN).astype(jnp.bfloat16)
    weight_grad = jnp.stack(grad_taps).reshape(3, 3, COUT, CIN)
    return (outputs, input_grad, weight_grad)
```

```python
import functools
import math

import jax
import jax.numpy as jnp
from jax import lax
from jax.experimental import pallas as pl
from jax.experimental.pallas import tpu as pltpu
from jax.sharding import PartitionSpec as P

MESH = pl.DeviceIdType.MESH
BF16 = jnp.bfloat16
F32 = jnp.float32

NX, NY, NZ = 4, 4, 8
LANES = 128

SEM_X = 0
SEM_W = 8
SEM_G = 12
SEM_T = 16
SEM_C = 18
SEM_DX = 22
SEM_DW = 30
SEM_OC = 34
SEM_O = 35
SEM_OH = 39
SEM_OT = 40
N_SEMS = 41


def kernel(
    norm,
    x_in, w_in, g_in,
    out_o, dx_o, dw_o,
    xg, wg, gg, x3, y3, dyn, wf, wb,
    pdx, rdx, acc, pdw, rdw, po, rk, ro, rh, ob, orx,
    ss, rs,
):
    chan = lax.axis_index("chan")
    filt = lax.axis_index("filt")
    x, k = lax.div(chan, 2), lax.rem(chan, 2)
    y, z = lax.div(filt, NZ), lax.rem(filt, NZ)

    def dev(dx, dk, dy, dz):
        return (dx * 2 + dk, dy * NZ + dz)

    def mod(v, n):
        return lax.rem(v + n, n)

    x_right, x_left = dev(mod(x + 1, NX), k, y, z), dev(mod(x - 1, NX), k, y, z)
    y_right, y_left = dev(x, k, mod(y + 1, NY), z), dev(x, k, mod(y - 1, NY), z)
    z_right, z_left = dev(x, k, y, mod(z + 1, NZ)), dev(x, k, y, mod(z - 1, NZ))
    other = dev(x, 1 - k, y, z)
    swap = dev(y, k, x, z)
    off_diag = x != y
    step = 2 * k - 1
    halo_to = dev(y, 1 - k, mod(x + step, NY), z)
    halo_from = dev(mod(y + step, NX), 1 - k, x, z)
    edge = dev(x, 1 - k, mod(y + step, NY), z)

    barrier = pltpu.get_barrier_semaphore()
    for peer in (
        x_right, x_left, y_right, y_left, z_right, z_left, other, halo_to, halo_from, edge,
    ):
        pl.semaphore_signal(barrier, inc=1, device_id=peer, device_id_type=MESH)

    @pl.when(off_diag)
    def _():
        pl.semaphore_signal(barrier, inc=1, device_id=swap, device_id_type=MESH)

    xg[z] = x_in[...]
    wg[y] = w_in[...]
    pl.semaphore_wait(barrier, jnp.where(off_diag, 11, 10))

    sent = []

    def rcopy(src, dst, idx, target):
        return pltpu.make_async_remote_copy(
            src_ref=src, dst_ref=dst, send_sem=ss.at[idx], recv_sem=rs.at[idx],
            device_id=target, device_id_type=MESH,
        )

    def push(src, dst, idx, target):
        copy = rcopy(src, dst, idx, target)
        copy.start()
        sent.append(copy)

    def landed(dst, idx):
        rcopy(dst, dst, idx, other).wait_recv()

    def gather(buf, own, pos, n, right, left, base, half):
        last = n // 2

        def send(s):
            for d in range(2):
                block = mod(pos - s + 1, n) if d == 0 else mod(pos + s - 1, n)
                src = own if s == 1 else buf.at[block]
                dst = buf.at[block]
                if s == last:
                    src, dst = half(src, d), half(dst, d)
                push(src, dst, base + d * last + s - 1, right if d == 0 else left)

        def recv(s):
            for d in range(2):
                block = mod(pos - s, n) if d == 0 else mod(pos + s, n)
                dst = buf.at[block]
                if s == last:
                    dst = half(dst, d)
                landed(dst, base + d * last + s - 1)

        return send, recv

    def scatter(part, got, pos, n, right, left, base, half):
        last = n // 2

        def dest(t, d):
            away = last + 1 - t
            return mod(pos + away, n) if d == 0 else mod(pos - away, n)

        def send(t):
            for d in range(2):
                src, dst = part(dest(t, d)), got.at[d, t - 1]
                if t == 1:
                    src, dst = half(src, d), half(dst, d)
                push(src, dst, base + d * last + t - 1, right if d == 0 else left)

        def recv(t):
            for d in range(2):
                dst = got.at[d, t - 1]
                if t == 1:
                    dst = half(dst, d)
                landed(dst, base + d * last + t - 1)

        def add(t):
            for d in range(2):
                into, term = part(dest(t + 1, d)), got.at[d, t - 1]
                if t == 1:
                    into, term = half(into, d), half(term, d)
                into[...] += term[...]

        def advance(t):
            recv(t)
            add(t)
            send(t + 1)

        return send, recv, advance

    first = lambda ref, d: ref.at[d]
    x_send, x_recv = gather(xg, x_in, z, NZ, z_right, z_left, SEM_X, first)
    w_send, w_recv = gather(
        wg, w_in, y, NY, y_right, y_left, SEM_W, lambda ref, d: ref.at[:, :, pl.ds(16 * d, 16)]
    )
    gk = gg.at[k]
    g_send, g_recv = gather(
        gk, gk.at[x], x, NX, x_right, x_left, SEM_G, lambda ref, d: ref.at[:, pl.ds(16 * d, 16)]
    )
    dx_send, dx_recv, dx_advance = scatter(
        lambda i: pdx.at[i + 1], rdx, z, NZ, z_right, z_left, SEM_DX, first
    )
    dw_send, dw_recv, dw_advance = scatter(
        lambda i: pdw.at[i], rdw, y, NY, y_right, y_left, SEM_DW, first
    )
    pk = po.at[k]
    o_send, o_recv, o_advance = scatter(
        lambda i: pk.at[i], ro, x, NX, x_right, x_left, SEM_O, first
    )

    main_dst = gg.at[k, y, pl.ds(1 - k, 8)]

    @pl.when(off_diag)
    def _():
        rcopy(g_in, main_dst, SEM_T, swap).start()

    @pl.when(jnp.logical_not(off_diag))
    def _():
        pltpu.make_async_copy(g_in, main_dst, rs.at[SEM_T]).start()

    push(g_in.at[7 * k], gg.at[1 - k, y, 8 * (1 - k)], SEM_T + 1, halo_to)
    w_send(1)
    x_send(1)

    own = gg.at[k, x, pl.ds(1 - k, 8)]

    @pl.when(off_diag)
    def _():
        rcopy(g_in, own, SEM_T, swap).wait_recv()

    @pl.when(jnp.logical_not(off_diag))
    def _():
        pltpu.make_async_copy(g_in, own, rs.at[SEM_T]).wait()

    landed(gg.at[k, x, 8 * k], SEM_T + 1)
    g_send(1)

    def core_send(i, b):
        push(gg.at[k, b], gg.at[k, b], SEM_C + i, other)

    blocks = (x, mod(x - 1, NX), mod(x + 1, NX), mod(x + 2, NX))
    core_send(0, blocks[0])
    w_recv(1)
    w_send(2)
    x_recv(1)
    x_send(2)
    g_recv(1)
    g_send(2)
    core_send(1, blocks[1])
    core_send(2, blocks[2])
    x_recv(2)
    x_send(3)
    w_recv(2)

    for b in range(NY):
        for i in range(3):
            for j in range(3):
                tap = wg[b, i, j]
                wf[i * 128 + b * 32 : i * 128 + b * 32 + 32, j * 128 : j * 128 + 128] = tap
                wb[j * 128 + b * 32 : j * 128 + b * 32 + 32, i * 128 : i * 128 + 128] = tap

    g_recv(2)
    core_send(3, blocks[3])
    x_recv(3)
    x_send(4)
    for i in range(4):
        landed(gg.at[1 - k, blocks[i]], SEM_C + i)

    col = lax.broadcasted_iota(jnp.int32, (LANES, LANES), 0)

    def shifts(v):
        before = jnp.where(col == 0, 0.0, pltpu.roll(v, 1, 0))
        after = jnp.where(col == LANES - 1, 0.0, pltpu.roll(v, LANES - 1, 0))
        return before.astype(BF16), after.astype(BF16)

    def y_row(q, carry):
        outside = jnp.logical_or(
            jnp.logical_and(q == 0, y == 0), jnp.logical_and(q == 17, y == NY - 1)
        )
        v = gg[lax.div(q, 9), :, lax.rem(q, 9)].reshape(LANES, LANES).astype(F32)
        v = jnp.where(outside, 0.0, v)
        at = pl.multiple_of(q * LANES, LANES)
        dyn[:, pl.ds(at, LANES)] = v.astype(BF16)
        t = v.T
        before, after = shifts(t)
        y3[pl.ds(at, LANES), 0:128] = after
        y3[pl.ds(at, LANES), 128:256] = t.astype(BF16)
        y3[pl.ds(at, LANES), 256:384] = before
        return carry

    lax.fori_loop(0, 18, y_row, 0)

    pdx[0] = jnp.zeros((2, LANES, LANES), F32)

    def dx_pair(t, carry):
        at = pl.multiple_of(t * 2 * LANES, 2 * LANES)
        r = jnp.dot(y3[pl.ds(at, 2 * LANES), :], wb[...], preferred_element_type=F32)
        r0, r1 = r[:LANES], r[LANES:]
        pdx[t, 0] += r0[:, 0:128]
        pdx[t, 1] += r0[:, 128:256] + r1[:, 0:128]
        pdx[t + 1, 0] = r0[:, 256:384] + r1[:, 128:256]
        pdx[t + 1, 1] = r1[:, 256:384]
        return carry

    lax.fori_loop(0, 9, dx_pair, 0)
    dx_send(1)

    x_recv(4)

    def x_row(r, carry):
        v16 = xg[lax.div(r, 2), lax.rem(r, 2)]
        before, after = shifts(v16.astype(F32))
        at = pl.multiple_of(r * LANES, LANES)
        x3[pl.ds(at, LANES), 0:128] = before
        x3[pl.ds(at, LANES), 128:256] = v16
        x3[pl.ds(at, LANES), 256:384] = after
        return carry

    lax.fori_loop(0, 16, x_row, 0)
    dx_advance(1)

    tile = (NX, 2, 16, LANES)
    po[0, :, :, 0] = jnp.zeros(tile, F32)
    po[0, :, :, 1] = jnp.zeros(tile, F32)

    def out_pair(t, carry):
        at = pl.multiple_of(t * 2 * LANES, 2 * LANES)
        r = lax.dot_general(
            wf[...], x3[pl.ds(at, 2 * LANES), :], (((1,), (1,)), ((), ())),
            preferred_element_type=F32,
        )
        r0, r1 = r[:, :LANES], r[:, LANES:]

        def row(q):
            return po.at[lax.div(q, 9), :, :, lax.rem(q, 9)]

        row(2 * t)[...] += r0[256:384].reshape(tile)
        row(2 * t + 1)[...] += (r0[128:256] + r1[256:384]).reshape(tile)
        row(2 * t + 2)[...] = (r0[0:128] + r1[128:256]).reshape(tile)
        row(2 * t + 3)[...] = r1[0:128].reshape(tile)
        return carry

    lax.fori_loop(0, 8, out_pair, 0)
    push(po.at[1 - k], rk, SEM_OC, other)
    dx_advance(2)

    acc[...] = jnp.zeros((384, 384), F32)

    def dw_rows(t, carry):
        at = pl.multiple_of(t * 4 * LANES, 4 * LANES)
        lhs = jnp.concatenate(
            [dyn[:, pl.ds(pl.multiple_of(at + (2 - i) * LANES, LANES), 4 * LANES)] for i in range(3)],
            axis=0,
        )
        acc[...] += jnp.dot(lhs, x3[pl.ds(at, 4 * LANES), :], preferred_element_type=F32)
        return carry

    lax.fori_loop(0, 4, dw_rows, 0)
    for b in range(NY):
        for h in range(2):
            for i in range(3):
                at = i * 128 + b * 32 + h * 16
                pdw[b, h, i] = acc[at : at + 16, :]
    dw_send(1)

    landed(rk, SEM_OC)
    for b in range(NX):
        pk.at[b][...] += rk[b]
    o_send(1)
    dx_advance(3)
    dw_advance(1)
    o_advance(1)

    dw_recv(2)
    for h in range(2):
        for i in range(3):
            total = (pdw[y, h, i] + rdw[0, 1, h, i] + rdw[1, 1, h, i]) * norm
            for j in range(3):
                dw_o[i, j, 16 * h : 16 * h + 16] = total[:, 128 * j : 128 * j + 128]

    o_recv(2)
    mine = po.at[k, x]
    for h in range(2):
        for q in range(9):
            mine[h, q] += ro[0, 1, h, q] + ro[1, 1, h, q]
    push(mine.at[:, 8 * k], rh, SEM_OH, edge)

    dx_recv(4)
    dx_o[...] = (pdx[z + 1] + rdx[0, 3] + rdx[1, 3]).astype(BF16)

    landed(rh, SEM_OH)
    inside = jnp.where(k == 0, y > 0, y < NY - 1)
    for h in range(2):
        mine[h, 1 + 6 * k + (1 - k) * 0] += jnp.where(inside, rh[h], 0.0)
        for q in range(8):
            ob[q, 16 * h : 16 * h + 16] = mine[h, q + 1 - k].astype(BF16)

    @pl.when(off_diag)
    def _():
        rcopy(ob, orx, SEM_OT, swap).start()
        rcopy(ob, orx, SEM_OT, swap).wait_recv()
        out_o[...] = orx[...]
        rcopy(ob, orx, SEM_OT, swap).wait_send()
        rcopy(g_in, main_dst, SEM_T, swap).wait_send()

    @pl.when(jnp.logical_not(off_diag))
    def _():
        out_o[...] = ob[...]

    for copy in sent:
        copy.wait_send()


def body(inputs, weights, cotangent):
    norm = 1.0 / math.sqrt(inputs.shape[0] * cotangent.shape[1] * 8 * inputs.shape[2])
    vmem = pl.BlockSpec(memory_space=pltpu.VMEM)
    out, dx, dw = pl.pallas_call(
        functools.partial(kernel, norm),
        out_shape=(
            jax.ShapeDtypeStruct((8, 32, 128), BF16),
            jax.ShapeDtypeStruct((2, 128, 128), BF16),
            jax.ShapeDtypeStruct((3, 3, 32, 128), F32),
        ),
        in_specs=[vmem] * 3,
        out_specs=[vmem] * 3,
        scratch_shapes=[
            pltpu.VMEM((8, 2, 128, 128), BF16),
            pltpu.VMEM((4, 3, 3, 32, 128), BF16),
            pltpu.VMEM((2, 4, 9, 32, 128), BF16),
            pltpu.VMEM((2048, 384), BF16),
            pltpu.VMEM((2304, 384), BF16),
            pltpu.VMEM((128, 2304), BF16),
            pltpu.VMEM((384, 384), BF16),
            pltpu.VMEM((384, 384), BF16),
            pltpu.VMEM((10, 2, 128, 128), F32),
            pltpu.VMEM((2, 4, 2, 128, 128), F32),
            pltpu.VMEM((384, 384), F32),
            pltpu.VMEM((4, 2, 3, 16, 384), F32),
            pltpu.VMEM((2, 2, 2, 3, 16, 384), F32),
            pltpu.VMEM((2, 4, 2, 9, 16, 128), F32),
            pltpu.VMEM((4, 2, 9, 16, 128), F32),
            pltpu.VMEM((2, 2, 2, 9, 16, 128), F32),
            pltpu.VMEM((2, 16, 128), F32),
            pltpu.VMEM((8, 32, 128), BF16),
            pltpu.VMEM((8, 32, 128), BF16),
            pltpu.SemaphoreType.DMA((N_SEMS,)),
            pltpu.SemaphoreType.DMA((N_SEMS,)),
        ],
        compiler_params=pltpu.CompilerParams(collective_id=0, has_side_effects=True),
        name="conv_layer",
    )(inputs[0], weights, cotangent[0])
    return out[None], dx[None], dw


def solution(mesh):
    return jax.shard_map(
        body,
        mesh=mesh,
        in_specs=(
            P(None, "filt", None, "chan"),
            P(None, None, "filt", "chan"),
            P(None, "chan", "filt", None),
        ),
        out_specs=(
            P(None, "chan", "filt", None),
            P(None, "filt", None, "chan"),
            P(None, None, "filt", "chan"),
        ),
        check_vma=False,
    )
```

```python
import functools
import math

import jax
import jax.numpy as jnp
from jax import lax
from jax.experimental import pallas as pl
from jax.experimental.pallas import tpu as pltpu
from jax.sharding import PartitionSpec as P

MESH = pl.DeviceIdType.MESH
BF16 = jnp.bfloat16
F32 = jnp.float32

NX, NY, NZ = 4, 4, 8
LANES = 128

SEM_X = 0
SEM_W = SEM_X + 8
SEM_T = SEM_W + 4
SEM_H = SEM_T + 4
SEM_C = SEM_H + 4
SEM_DX = SEM_C + 4
SEM_DW = SEM_DX + 16
SEM_O = SEM_DW + 8
SEM_OC = SEM_O + 8
SEM_OM = SEM_OC + 1
SEM_OE = SEM_OM + 1
SEM_OH = SEM_OE + 1
N_SEMS = SEM_OH + 1


def kernel(
    norm,
    x_in, w_in, g_in,
    out_o, dx_o, dw_o,
    gin, xg, wg, gg, x3, y3, dyn, wf, wb,
    pdx, rdx, acc, pdw, rdw, po, rk, ro, ob, orx, oe, oh,
    ss, rs, ls,
):
    chan = lax.axis_index("chan")
    filt = lax.axis_index("filt")
    x, k = lax.div(chan, 2), lax.rem(chan, 2)
    y, z = lax.div(filt, NZ), lax.rem(filt, NZ)

    def dev(dx, dk, dy, dz):
        return (dx * 2 + dk, dy * NZ + dz)

    def mod(v, n):
        return lax.rem(v + n, n)

    x_right, x_left = dev(mod(x + 1, NX), k, y, z), dev(mod(x - 1, NX), k, y, z)
    y_right, y_left = dev(x, k, mod(y + 1, NY), z), dev(x, k, mod(y - 1, NY), z)
    z_right, z_left = dev(x, k, y, mod(z + 1, NZ)), dev(x, k, y, mod(z - 1, NZ))
    other = dev(x, 1 - k, y, z)
    swap = dev(y, k, x, z)
    off_diag = x != y
    step = 2 * k - 1
    out_halo_to = dev(mod(y + step, NX), 1 - k, x, z)
    out_halo_from = dev(y, 1 - k, mod(x + step, NY), z)

    loads = [
        pltpu.make_async_copy(g_in, gin, ls.at[0]),
        pltpu.make_async_copy(x_in, xg.at[z], ls.at[1]),
        pltpu.make_async_copy(w_in, wg.at[y], ls.at[2]),
    ]
    for load in loads:
        load.start()

    barrier = pltpu.get_barrier_semaphore()

    def greet(peer):
        pl.semaphore_signal(barrier, inc=1, device_id=peer, device_id_type=MESH)

    for i in range(NY):
        b = mod(y + i, NY)
        greet(dev(mod(y + step, NX), 1 - k, b, z))
        if i:
            greet(dev(y, k, mod(x + i, NY), z))
    for peer in (x_right, x_left, y_right, y_left, z_right, z_left, other, out_halo_from):
        greet(peer)

    @pl.when(off_diag)
    def _():
        greet(swap)

    pdx[...] = jnp.zeros_like(pdx)
    po[...] = jnp.zeros_like(po)
    pl.semaphore_wait(barrier, jnp.where(off_diag, 16, 15))
    for load in loads:
        load.wait()

    sent = []

    def rcopy(src, dst, idx, target):
        return pltpu.make_async_remote_copy(
            src_ref=src, dst_ref=dst, send_sem=ss.at[idx], recv_sem=rs.at[idx],
            device_id=target, device_id_type=MESH,
        )

    def push(src, dst, idx, target):
        copy = rcopy(src, dst, idx, target)
        copy.start()
        sent.append(copy)

    def landed(dst, idx):
        rcopy(dst, dst, idx, other).wait_recv()

    def gather(buf, pos, n, right, left, base, half):
        last = n // 2

        def send(s):
            for d in range(2):
                ref = buf.at[mod(pos - s + 1, n) if d == 0 else mod(pos + s - 1, n)]
                if s == last:
                    ref = half(ref, d)
                push(ref, ref, base + d * last + s - 1, right if d == 0 else left)

        def recv(s):
            for d in range(2):
                ref = buf.at[mod(pos - s, n) if d == 0 else mod(pos + s, n)]
                if s == last:
                    ref = half(ref, d)
                landed(ref, base + d * last + s - 1)

        return send, recv

    def scatter(part, got, pos, n, right, left, base):
        last = n // 2

        def dest(t, d):
            away = last + 1 - t
            return mod(pos + away, n) if d == 0 else mod(pos - away, n)

        def sem(t, d, piece):
            return base + (d * last + t - 1) * 2 + piece

        def send(t, d, piece):
            push(
                part(dest(t, d)).at[piece], got.at[d, t - 1, piece], sem(t, d, piece),
                right if d == 0 else left,
            )

        def start():
            for d in range(2):
                send(1, d, d)

        def start_free():
            for d in range(2):
                send(2, d, 1 - d)

        def advance(t):
            for turn in (1, 0) if t > 1 else (0,):
                for d in range(2):
                    piece = 1 - d if turn else d
                    landed(got.at[d, t - 1, piece], sem(t, d, piece))
                    part(dest(t + 1, d)).at[piece][...] += got[d, t - 1, piece]
                    send(t + 1, d, piece)

        def finish():
            for d in range(2):
                for piece in range(2):
                    landed(got.at[d, last - 1, piece], sem(last, d, piece))

        return start, start_free, advance, finish

    x_send, x_recv = gather(xg, z, NZ, z_right, z_left, SEM_X, lambda ref, d: ref.at[d])
    w_send, w_recv = gather(
        wg, y, NY, y_right, y_left, SEM_W, lambda ref, d: ref.at[:, :, pl.ds(16 * d, 16)]
    )
    dx_start, dx_free, dx_advance, dx_finish = scatter(
        lambda i: pdx.at[i + 1], rdx, z, NZ, z_right, z_left, SEM_DX
    )
    dw_start, dw_free, dw_advance, dw_finish = scatter(
        lambda i: pdw.at[i], rdw, y, NY, y_right, y_left, SEM_DW
    )
    pk = po.at[k]
    o_start, o_free, o_advance, o_finish = scatter(
        lambda i: pk.at[i], ro, x, NX, x_right, x_left, SEM_O
    )

    def main_copy(i):
        target = dev(mod(x + i, NX), k, x, z)
        return pltpu.make_async_remote_copy(
            src_ref=gin, dst_ref=gg.at[k, y, pl.ds(1 - k, 8)],
            send_sem=ss.at[SEM_T + i], recv_sem=rs.at[SEM_T + y],
            device_id=target, device_id_type=MESH,
        )

    def self_copy():
        return pltpu.make_async_copy(gin, gg.at[k, y, pl.ds(1 - k, 8)], ls.at[0])

    for i in (2, 1, 3):
        main_copy(i).start()

    @pl.when(off_diag)
    def _():
        main_copy(0).start()

    @pl.when(jnp.logical_not(off_diag))
    def _():
        self_copy().start()

    x_send(1)
    w_send(1)
    for i in range(NX):
        copy = pltpu.make_async_remote_copy(
            src_ref=gin.at[7 * k], dst_ref=gg.at[1 - k, y, 8 * (1 - k)],
            send_sem=ss.at[SEM_H + i], recv_sem=rs.at[SEM_H + y],
            device_id=dev(mod(x + i, NX), 1 - k, mod(x + step, NY), z), device_id_type=MESH,
        )
        copy.start()
        sent.append(copy)

    w_recv(1)
    w_send(2)
    x_recv(1)
    x_send(2)

    def cot_block(i):
        b = mod(x + i, NY)
        ref = gg.at[k, b, pl.ds(1 - k, 8)]
        if i:
            landed(ref, SEM_T + b)
        else:

            @pl.when(off_diag)
            def _():
                landed(ref, SEM_T + b)

            @pl.when(jnp.logical_not(off_diag))
            def _():
                self_copy().wait()

        landed(gg.at[k, b, 8 * k], SEM_H + b)
        push(gg.at[k, b], gg.at[k, b], SEM_C + i, other)

    for i in (0, 1, 3, 2):
        cot_block(i)
    x_recv(2)
    x_send(3)

    col = lax.broadcasted_iota(jnp.int32, (LANES, LANES), 0)

    def shifts(v):
        before = jnp.where(col == 0, 0.0, pltpu.roll(v, 1, 0))
        after = jnp.where(col == LANES - 1, 0.0, pltpu.roll(v, LANES - 1, 0))
        return before.astype(BF16), after.astype(BF16)

    def y_rows(half):
        def row(ql):
            q = half * 9 + ql
            outside = jnp.logical_or(
                jnp.logical_and(q == 0, y == 0), jnp.logical_and(q == 17, y == NY - 1)
            )
            v = gg[half, :, ql].reshape(LANES, LANES).astype(F32)
            v = jnp.where(outside, 0.0, v)
            at = pl.multiple_of(q * LANES, LANES)
            dyn[:, pl.ds(at, LANES)] = v.astype(BF16)
            t = v.T
            before, after = shifts(t)
            y3[pl.ds(at, LANES), 0:128] = after
            y3[pl.ds(at, LANES), 128:256] = t.astype(BF16)
            y3[pl.ds(at, LANES), 256:384] = before

        def rows(g, carry):
            for u in range(3):
                row(g * 3 + u)
            return carry

        lax.fori_loop(0, 3, rows, 0)

    y_rows(k)
    w_recv(2)
    for b in range(NY):
        for i in range(3):
            for j in range(3):
                tap = wg[b, i, j]
                wf[i * 128 + b * 32 : i * 128 + b * 32 + 32, j * 128 : j * 128 + 128] = tap
                wb[j * 128 + b * 32 : j * 128 + b * 32 + 32, i * 128 : i * 128 + 128] = tap

    for i in (0, 1, 3, 2):
        landed(gg.at[1 - k, mod(x + i, NY)], SEM_C + i)
    y_rows(1 - k)

    far = mod(z + NZ // 2, NZ)

    def dx_pair(i):
        t = mod(far + i, 9)
        at = pl.multiple_of(t * 2 * LANES, 2 * LANES)
        r = jnp.dot(y3[pl.ds(at, 2 * LANES), :], wb[...], preferred_element_type=F32)
        r0, r1 = r[:LANES], r[LANES:]
        pdx[t, 0] += r0[:, 0:128]
        pdx[t, 1] += r0[:, 128:256] + r1[:, 0:128]
        pdx[t + 1, 0] += r0[:, 256:384] + r1[:, 128:256]
        pdx[t + 1, 1] += r1[:, 256:384]

    for i in range(2):
        dx_pair(i)
    dx_start()
    x_recv(3)
    x_send(4)
    for i in range(2, 9):
        dx_pair(i)
    dx_free()

    x_recv(4)

    def x_rows(g, carry):
        for u in range(2):
            v16 = xg[g, u]
            before, after = shifts(v16.astype(F32))
            at = pl.multiple_of((g * 2 + u) * LANES, LANES)
            x3[pl.ds(at, LANES), 0:128] = before
            x3[pl.ds(at, LANES), 128:256] = v16
            x3[pl.ds(at, LANES), 256:384] = after
        return carry

    lax.fori_loop(0, 8, x_rows, 0)

    tile = (NX, 2, 16, LANES)

    def out_pair(i):
        t = (1 - k) * 7 + step * i
        at = pl.multiple_of(t * 2 * LANES, 2 * LANES)
        r = lax.dot_general(
            wf[...], x3[pl.ds(at, 2 * LANES), :], (((1,), (1,)), ((), ())),
            preferred_element_type=F32,
        )
        r0, r1 = r[:, :LANES], r[:, LANES:]

        def row(q):
            return po.at[lax.div(q, 9), :, :, lax.rem(q, 9)]

        row(2 * t)[...] += r0[256:384].reshape(tile)
        row(2 * t + 1)[...] += (r0[128:256] + r1[256:384]).reshape(tile)
        row(2 * t + 2)[...] += (r0[0:128] + r1[128:256]).reshape(tile)
        row(2 * t + 3)[...] += r1[0:128].reshape(tile)

    for i in range(5):
        out_pair(i)
    push(po.at[1 - k], rk, SEM_OC, other)
    dx_advance(1)
    for i in range(5, 8):
        out_pair(i)

    landed(rk, SEM_OC)
    b = mod(x + 2, NX)
    pk.at[b][...] += rk[b]
    o_start()
    for i in (1, 3, 0):
        b = mod(x + i, NX)
        pk.at[b][...] += rk[b]
    o_free()

    def dw_rows(t):
        at = t * 4 * LANES
        lhs = jnp.concatenate(
            [dyn[:, at + (2 - i) * LANES : at + (6 - i) * LANES] for i in range(3)], axis=0
        )
        return jnp.dot(lhs, x3[at : at + 4 * LANES, :], preferred_element_type=F32)

    acc[...] = dw_rows(0)
    acc[...] += dw_rows(1)
    dx_advance(2)
    acc[...] += dw_rows(2)
    acc[...] += dw_rows(3)
    for b in range(NY):
        for h in range(2):
            for i in range(3):
                at = i * 128 + b * 32 + h * 16
                pdw[b, h, i] = acc[at : at + 16, :]
    dw_start()
    dw_free()

    o_advance(1)
    dx_advance(3)
    dw_advance(1)

    o_finish()
    mine = po.at[k, x]
    for h in range(2):
        for q in range(9):
            mine[h, q] += ro[0, 1, h, q] + ro[1, 1, h, q]
    edge = mine.at[:, 7 * k + 1 - k]
    push(mine.at[:, 8 * k], oh, SEM_OH, out_halo_to)
    for h in range(2):
        for q in range(7):
            ob[q, 16 * h : 16 * h + 16] = mine[h, q + 2 * (1 - k)].astype(BF16)

    def out_copies():
        return (rcopy(ob, orx, SEM_OM, swap), rcopy(edge, oe, SEM_OE, swap))

    def out_stays():
        return (
            pltpu.make_async_copy(ob, orx, ls.at[0]), pltpu.make_async_copy(edge, oe, ls.at[1])
        )

    @pl.when(off_diag)
    def _():
        for copy in out_copies():
            copy.start()

    @pl.when(jnp.logical_not(off_diag))
    def _():
        for copy in out_stays():
            copy.start()

    dx_finish()
    dx_o[...] = (pdx[z + 1] + rdx[0, 3] + rdx[1, 3]).astype(BF16)

    dw_finish()
    for h in range(2):
        for i in range(3):
            total = (pdw[y, h, i] + rdw[0, 1, h, i] + rdw[1, 1, h, i]) * norm
            for j in range(3):
                dw_o[i, j, 16 * h : 16 * h + 16] = total[:, 128 * j : 128 * j + 128]

    @pl.when(off_diag)
    def _():
        for copy in out_copies():
            copy.wait()
        main_copy(0).wait_send()

    @pl.when(jnp.logical_not(off_diag))
    def _():
        for copy in out_stays():
            copy.wait()

    landed(oh, SEM_OH)
    inside = jnp.where(k == 0, x > 0, x < NX - 1)
    out_o[pl.ds(1 - k, 7)] = orx[...]
    for h in range(2):
        row = oe[h] + jnp.where(inside, oh[h], 0.0)
        out_o[7 * k, 16 * h : 16 * h + 16] = row.astype(BF16)

    for i in range(1, NX):
        main_copy(i).wait_send()
    for copy in sent:
        copy.wait_send()


def body(inputs, weights, cotangent):
    norm = 1.0 / math.sqrt(inputs.shape[0] * cotangent.shape[1] * 8 * inputs.shape[2])
    vmem = pl.BlockSpec(memory_space=pltpu.VMEM)
    hbm = pl.BlockSpec(memory_space=pl.ANY)
    out, dx, dw = pl.pallas_call(
        functools.partial(kernel, norm),
        out_shape=(
            jax.ShapeDtypeStruct((8, 32, 128), BF16),
            jax.ShapeDtypeStruct((2, 128, 128), BF16),
            jax.ShapeDtypeStruct((3, 3, 32, 128), F32),
        ),
        in_specs=[hbm] * 3,
        out_specs=[vmem] * 3,
        scratch_shapes=[
            pltpu.VMEM((8, 32, 128), BF16),
            pltpu.VMEM((8, 2, 128, 128), BF16),
            pltpu.VMEM((4, 3, 3, 32, 128), BF16),
            pltpu.VMEM((2, 4, 9, 32, 128), BF16),
            pltpu.VMEM((2048, 384), BF16),
            pltpu.VMEM((2304, 384), BF16),
            pltpu.VMEM((128, 2304), BF16),
            pltpu.VMEM((384, 384), BF16),
            pltpu.VMEM((384, 384), BF16),
            pltpu.VMEM((10, 2, 128, 128), F32),
            pltpu.VMEM((2, 4, 2, 128, 128), F32),
            pltpu.VMEM((384, 384), F32),
            pltpu.VMEM((4, 2, 3, 16, 384), F32),
            pltpu.VMEM((2, 2, 2, 3, 16, 384), F32),
            pltpu.VMEM((2, 4, 2, 9, 16, 128), F32),
            pltpu.VMEM((4, 2, 9, 16, 128), F32),
            pltpu.VMEM((2, 2, 2, 9, 16, 128), F32),
            pltpu.VMEM((7, 32, 128), BF16),
            pltpu.VMEM((7, 32, 128), BF16),
            pltpu.VMEM((2, 16, 128), F32),
            pltpu.VMEM((2, 16, 128), F32),
            pltpu.SemaphoreType.DMA((N_SEMS,)),
            pltpu.SemaphoreType.DMA((N_SEMS,)),
            pltpu.SemaphoreType.DMA((3,)),
        ],
        compiler_params=pltpu.CompilerParams(collective_id=0, has_side_effects=True),
        name="conv_layer",
    )(inputs[0], weights, cotangent[0])
    return out[None], dx[None], dw


def solution(mesh):
    return jax.shard_map(
        body,
        mesh=mesh,
        in_specs=(
            P(None, "filt", None, "chan"),
            P(None, None, "filt", "chan"),
            P(None, "chan", "filt", None),
        ),
        out_specs=(
            P(None, "chan", "filt", None),
            P(None, "filt", None, "chan"),
            P(None, None, "filt", "chan"),
        ),
        check_vma=False,
    )
```

```python
import functools
import math

import jax
import jax.numpy as jnp
from jax import lax
from jax.experimental import pallas as pl
from jax.experimental.pallas import tpu as pltpu
from jax.sharding import PartitionSpec as P

MESH = pl.DeviceIdType.MESH
BF16 = jnp.bfloat16
F32 = jnp.float32

NX, NY, NZ = 4, 4, 8
LANES = 128

SEM_X = 0
SEM_W = SEM_X + 16
SEM_T = SEM_W + 4
SEM_H = SEM_T + 4
SEM_C = SEM_H + 4
SEM_DX = SEM_C + 4
SEM_DW = SEM_DX + 16
SEM_O = SEM_DW + 8
SEM_OC = SEM_O + 8
SEM_OM = SEM_OC + 4
SEM_OE = SEM_OM + 1
SEM_OH = SEM_OE + 1
N_SEMS = SEM_OH + 1


def kernel(
    norm,
    x_in, w_in, g_in,
    out_o, dx_o, dw_o,
    gin, xg, wg, gg, x3, y3, dyn, wf, wb,
    pdx, rdx, acc, pdw, rdw, po, rk, ro, ob, orx, oe, oh,
    ss, rs, ls,
):
    chan = lax.axis_index("chan")
    filt = lax.axis_index("filt")
    x, k = lax.div(chan, 2), lax.rem(chan, 2)
    y, z = lax.div(filt, NZ), lax.rem(filt, NZ)

    def dev(dx, dk, dy, dz):
        return (dx * 2 + dk, dy * NZ + dz)

    def mod(v, n):
        return lax.rem(v + n, n)

    x_right, x_left = dev(mod(x + 1, NX), k, y, z), dev(mod(x - 1, NX), k, y, z)
    y_right, y_left = dev(x, k, mod(y + 1, NY), z), dev(x, k, mod(y - 1, NY), z)
    z_right, z_left = dev(x, k, y, mod(z + 1, NZ)), dev(x, k, y, mod(z - 1, NZ))
    other = dev(x, 1 - k, y, z)
    swap = dev(y, k, x, z)
    off_diag = x != y
    step = 2 * k - 1
    out_halo_to = dev(mod(y + step, NX), 1 - k, x, z)
    out_halo_from = dev(y, 1 - k, mod(x + step, NY), z)

    loads = [
        pltpu.make_async_copy(g_in, gin, ls.at[0]),
        pltpu.make_async_copy(x_in, xg.at[z], ls.at[1]),
        pltpu.make_async_copy(w_in, wg.at[y], ls.at[2]),
    ]
    for load in loads:
        load.start()

    barrier = pltpu.get_barrier_semaphore()

    def greet(peer):
        pl.semaphore_signal(barrier, inc=1, device_id=peer, device_id_type=MESH)

    for i in range(NY):
        b = mod(y + i, NY)
        greet(dev(mod(y + step, NX), 1 - k, b, z))
        if i:
            greet(dev(y, k, mod(x + i, NY), z))
    for peer in (x_right, x_left, y_right, y_left, z_right, z_left, other, out_halo_from):
        greet(peer)

    @pl.when(off_diag)
    def _():
        greet(swap)

    pdx[...] = jnp.zeros_like(pdx)
    po[...] = jnp.zeros_like(po)
    pl.semaphore_wait(barrier, jnp.where(off_diag, 16, 15))
    for load in loads:
        load.wait()

    sent = []

    def rcopy(src, dst, idx, target):
        return pltpu.make_async_remote_copy(
            src_ref=src, dst_ref=dst, send_sem=ss.at[idx], recv_sem=rs.at[idx],
            device_id=target, device_id_type=MESH,
        )

    def push(src, dst, idx, target):
        copy = rcopy(src, dst, idx, target)
        copy.start()
        sent.append(copy)

    def landed(dst, idx):
        rcopy(dst, dst, idx, other).wait_recv()

    def gather(buf, pos, n, right, left, base, cut, pieces):
        last = n // 2

        def copy_at(s, d, piece, hops):
            ref = buf.at[mod(pos - s + hops, n) if d == 0 else mod(pos + s - hops, n)]
            if pieces == 2 or s == last:
                ref = cut(ref, piece)
            return ref, base + ((d * last + s - 1) * pieces + (piece if pieces == 2 else 0))

        def send(s, d, piece):
            ref, idx = copy_at(s, d, piece, 1)
            push(ref, ref, idx, right if d == 0 else left)

        def forward(s):
            for turn in range(pieces if s < last else 1):
                for d in range(2):
                    piece = 1 - d if turn else d
                    if s:
                        ref, idx = copy_at(s, d, piece, 0)
                        landed(ref, idx)
                    if s + 1 < last or s + 1 == last and turn == 0:
                        send(s + 1, d, piece)

        return forward

    def scatter(part, got, pos, n, right, left, base):
        last = n // 2

        def dest(t, d):
            away = last + 1 - t
            return mod(pos + away, n) if d == 0 else mod(pos - away, n)

        def sem(t, d, piece):
            return base + (d * last + t - 1) * 2 + piece

        def send(t, d, piece):
            push(
                part(dest(t, d)).at[piece], got.at[d, t - 1, piece], sem(t, d, piece),
                right if d == 0 else left,
            )

        def start():
            for d in range(2):
                send(1, d, d)

        def start_free():
            for d in range(2):
                send(2, d, 1 - d)

        def advance(t, free=False):
            for d in range(2):
                piece = 1 - d if free else d
                landed(got.at[d, t - 1, piece], sem(t, d, piece))
                part(dest(t + 1, d)).at[piece][...] += got[d, t - 1, piece]
                send(t + 1, d, piece)

        def finish():
            for d in range(2):
                for piece in range(2):
                    landed(got.at[d, last - 1, piece], sem(last, d, piece))

        return start, start_free, advance, finish

    x_forward = gather(xg, z, NZ, z_right, z_left, SEM_X, lambda ref, d: ref.at[d], 2)
    w_forward = gather(
        wg, y, NY, y_right, y_left, SEM_W, lambda ref, d: ref.at[:, :, pl.ds(16 * d, 16)], 1
    )
    dx_start, dx_free, dx_advance, dx_finish = scatter(
        lambda i: pdx.at[i + 1], rdx, z, NZ, z_right, z_left, SEM_DX
    )
    dw_start, dw_free, dw_advance, dw_finish = scatter(
        lambda i: pdw.at[i], rdw, y, NY, y_right, y_left, SEM_DW
    )
    pk = po.at[k]
    o_start, o_free, o_advance, o_finish = scatter(
        lambda i: pk.at[i], ro, x, NX, x_right, x_left, SEM_O
    )

    def main_copy(i):
        target = dev(mod(x + i, NX), k, x, z)
        return pltpu.make_async_remote_copy(
            src_ref=gin, dst_ref=gg.at[k, y, pl.ds(1 - k, 8)],
            send_sem=ss.at[SEM_T + i], recv_sem=rs.at[SEM_T + y],
            device_id=target, device_id_type=MESH,
        )

    def self_copy():
        return pltpu.make_async_copy(gin, gg.at[k, y, pl.ds(1 - k, 8)], ls.at[0])

    w_forward(0)
    for i in (2, 1, 3):
        main_copy(i).start()

    @pl.when(off_diag)
    def _():
        main_copy(0).start()

    @pl.when(jnp.logical_not(off_diag))
    def _():
        self_copy().start()

    for i in range(NX):
        copy = pltpu.make_async_remote_copy(
            src_ref=gin.at[7 * k], dst_ref=gg.at[1 - k, y, 8 * (1 - k)],
            send_sem=ss.at[SEM_H + i], recv_sem=rs.at[SEM_H + y],
            device_id=dev(mod(x + i, NX), 1 - k, mod(x + step, NY), z), device_id_type=MESH,
        )
        copy.start()
        sent.append(copy)

    def cot_block(i):
        b = mod(x + i, NY)
        ref = gg.at[k, b, pl.ds(1 - k, 8)]
        if i:
            landed(ref, SEM_T + b)
        else:

            @pl.when(off_diag)
            def _():
                landed(ref, SEM_T + b)

            @pl.when(jnp.logical_not(off_diag))
            def _():
                self_copy().wait()

        landed(gg.at[k, b, 8 * k], SEM_H + b)
        push(gg.at[k, b], gg.at[k, b], SEM_C + i, other)

    col = lax.broadcasted_iota(jnp.int32, (LANES, LANES), 0)

    def shifts(v):
        before = jnp.where(col == 0, 0.0, pltpu.roll(v, 1, 0))
        after = jnp.where(col == LANES - 1, 0.0, pltpu.roll(v, LANES - 1, 0))
        return before.astype(BF16), after.astype(BF16)

    def y_rows(half):
        def row(ql):
            q = half * 9 + ql
            outside = jnp.logical_or(
                jnp.logical_and(q == 0, y == 0), jnp.logical_and(q == 17, y == NY - 1)
            )
            v = gg[half, :, ql].reshape(LANES, LANES).astype(F32)
            v = jnp.where(outside, 0.0, v)
            at = pl.multiple_of(q * LANES, LANES)
            dyn[:, pl.ds(at, LANES)] = v.astype(BF16)
            t = v.T
            before, after = shifts(t)
            y3[pl.ds(at, LANES), 0:128] = after
            y3[pl.ds(at, LANES), 128:256] = t.astype(BF16)
            y3[pl.ds(at, LANES), 256:384] = before

        def rows(g, carry):
            for u in range(3):
                row(g * 3 + u)
            return carry

        lax.fori_loop(0, 3, rows, 0)

    def x_block(i):
        block = mod(z + i, NZ)
        for u in range(2):
            v16 = xg[block, u]
            before, after = shifts(v16.astype(F32))
            at = pl.multiple_of((block * 2 + u) * LANES, LANES)
            x3[pl.ds(at, LANES), 0:128] = before
            x3[pl.ds(at, LANES), 128:256] = v16
            x3[pl.ds(at, LANES), 256:384] = after

    far = mod(z + NZ // 2, NZ)

    def dx_pair(i):
        t = mod(far + i, 9)
        at = pl.multiple_of(t * 2 * LANES, 2 * LANES)
        r = jnp.dot(y3[pl.ds(at, 2 * LANES), :], wb[...], preferred_element_type=F32)
        r0, r1 = r[:LANES], r[LANES:]
        pdx[t, 0] += r0[:, 0:128]
        pdx[t, 1] += r0[:, 128:256] + r1[:, 0:128]
        pdx[t + 1, 0] += r0[:, 256:384] + r1[:, 128:256]
        pdx[t + 1, 1] += r1[:, 256:384]

    tile = (NX, 2, 16, LANES)

    def out_pair(i):
        t = mod(z + i, NZ)
        at = pl.multiple_of(t * 2 * LANES, 2 * LANES)
        r = lax.dot_general(
            wf[...], x3[pl.ds(at, 2 * LANES), :], (((1,), (1,)), ((), ())),
            preferred_element_type=F32,
        )
        r0, r1 = r[:, :LANES], r[:, LANES:]

        def row(q):
            return po.at[lax.div(q, 9), :, :, lax.rem(q, 9)]

        row(2 * t)[...] += r0[256:384].reshape(tile)
        row(2 * t + 1)[...] += (r0[128:256] + r1[256:384]).reshape(tile)
        row(2 * t + 2)[...] += (r0[0:128] + r1[128:256]).reshape(tile)
        row(2 * t + 3)[...] += r1[0:128].reshape(tile)

    def dw_rows(t):
        at = t * 4 * LANES
        lhs = jnp.concatenate(
            [dyn[:, at + (2 - i) * LANES : at + (6 - i) * LANES] for i in range(3)], axis=0
        )
        return jnp.dot(lhs, x3[at : at + 4 * LANES, :], preferred_element_type=F32)

    x_forward(0)
    x_block(0)
    x_forward(1)
    x_block(1)
    x_block(-1)
    w_forward(1)
    x_forward(2)
    x_block(2)
    x_block(-2)
    for i in (0, 1, 3, 2):
        cot_block(i)
    y_rows(k)
    w_forward(2)
    for b in range(NY):
        for i in range(3):
            for j in range(3):
                tap = wg[b, i, j]
                wf[i * 128 + b * 32 : i * 128 + b * 32 + 32, j * 128 : j * 128 + 128] = tap
                wb[j * 128 + b * 32 : j * 128 + b * 32 + 32, i * 128 : i * 128 + 128] = tap

    for i in (0, 1, -1):
        out_pair(i)
    for i in (0, 1, 3, 2):
        landed(gg.at[1 - k, mod(x + i, NY)], SEM_C + i)
    y_rows(1 - k)

    for i in range(2):
        dx_pair(i)
    dx_start()
    x_forward(3)
    for i in range(2, 9):
        dx_pair(i)
    dx_free()
    for i in (2, -2):
        out_pair(i)
    for i in (3, -3):
        x_block(i)
        out_pair(i)
    x_forward(4)
    x_block(4)
    out_pair(4)
    for i in (2, 1, 3, 0):
        b = mod(x + i, NX)
        push(po.at[1 - k, b], rk.at[b], SEM_OC + i, other)
    dx_advance(1)
    acc[...] = dw_rows(0)
    acc[...] += dw_rows(1)

    def core_sum(i):
        b = mod(x + i, NX)
        landed(rk.at[b], SEM_OC + i)
        pk.at[b][...] += rk[b]

    core_sum(2)
    o_start()
    for i in (1, 3):
        core_sum(i)
    o_free()
    core_sum(0)
    dx_advance(2, free=True)
    acc[...] += dw_rows(2)
    acc[...] += dw_rows(3)
    for b in range(NY):
        for h in range(2):
            for i in range(3):
                at = i * 128 + b * 32 + h * 16
                pdw[b, h, i] = acc[at : at + 16, :]
    dw_start()
    dw_free()
    dx_advance(2)
    o_advance(1)
    dx_advance(3, free=True)
    dw_advance(1)
    dx_advance(3)

    o_finish()
    mine = po.at[k, x]
    for h in range(2):
        for q in range(9):
            mine[h, q] += ro[0, 1, h, q] + ro[1, 1, h, q]
    edge = mine.at[:, 7 * k + 1 - k]
    push(mine.at[:, 8 * k], oh, SEM_OH, out_halo_to)
    for h in range(2):
        for q in range(7):
            ob[q, 16 * h : 16 * h + 16] = mine[h, q + 2 * (1 - k)].astype(BF16)

    def out_copies():
        return (rcopy(ob, orx, SEM_OM, swap), rcopy(edge, oe, SEM_OE, swap))

    def out_stays():
        return (
            pltpu.make_async_copy(ob, orx, ls.at[0]), pltpu.make_async_copy(edge, oe, ls.at[1])
        )

    @pl.when(off_diag)
    def _():
        for copy in out_copies():
            copy.start()

    @pl.when(jnp.logical_not(off_diag))
    def _():
        for copy in out_stays():
            copy.start()

    dx_finish()
    dx_o[...] = (pdx[z + 1] + rdx[0, 3] + rdx[1, 3]).astype(BF16)

    dw_finish()
    for h in range(2):
        for i in range(3):
            total = (pdw[y, h, i] + rdw[0, 1, h, i] + rdw[1, 1, h, i]) * norm
            for j in range(3):
                dw_o[i, j, 16 * h : 16 * h + 16] = total[:, 128 * j : 128 * j + 128]

    @pl.when(off_diag)
    def _():
        for copy in out_copies():
            copy.wait()
        main_copy(0).wait_send()

    @pl.when(jnp.logical_not(off_diag))
    def _():
        for copy in out_stays():
            copy.wait()

    landed(oh, SEM_OH)
    inside = jnp.where(k == 0, x > 0, x < NX - 1)
    out_o[pl.ds(1 - k, 7)] = orx[...]
    for h in range(2):
        row = oe[h] + jnp.where(inside, oh[h], 0.0)
        out_o[7 * k, 16 * h : 16 * h + 16] = row.astype(BF16)

    for i in range(1, NX):
        main_copy(i).wait_send()
    for copy in sent:
        copy.wait_send()


def place(*refs):
    sems = refs[6]
    copies = [pltpu.make_async_copy(refs[i], refs[i + 3], sems.at[i]) for i in range(3)]
    for copy in copies:
        copy.start()
    for copy in copies:
        copy.wait()


def body(inputs, weights, cotangent):
    norm = 1.0 / math.sqrt(inputs.shape[0] * cotangent.shape[1] * 8 * inputs.shape[2])
    vmem = pl.BlockSpec(memory_space=pltpu.VMEM)
    hbm = pl.BlockSpec(memory_space=pl.ANY)
    out, dx, dw = pl.pallas_call(
        functools.partial(kernel, norm),
        out_shape=(
            pltpu.VMEM((8, 32, 128), BF16),
            pltpu.VMEM((2, 128, 128), BF16),
            pltpu.VMEM((3, 3, 32, 128), F32),
        ),
        in_specs=[hbm] * 3,
        out_specs=[vmem] * 3,
        scratch_shapes=[
            pltpu.VMEM((8, 32, 128), BF16),
            pltpu.VMEM((8, 2, 128, 128), BF16),
            pltpu.VMEM((4, 3, 3, 32, 128), BF16),
            pltpu.VMEM((2, 4, 9, 32, 128), BF16),
            pltpu.VMEM((2048, 384), BF16),
            pltpu.VMEM((2304, 384), BF16),
            pltpu.VMEM((128, 2304), BF16),
            pltpu.VMEM((384, 384), BF16),
            pltpu.VMEM((384, 384), BF16),
            pltpu.VMEM((10, 2, 128, 128), F32),
            pltpu.VMEM((2, 4, 2, 128, 128), F32),
            pltpu.VMEM((384, 384), F32),
            pltpu.VMEM((4, 2, 3, 16, 384), F32),
            pltpu.VMEM((2, 2, 2, 3, 16, 384), F32),
            pltpu.VMEM((2, 4, 2, 9, 16, 128), F32),
            pltpu.VMEM((4, 2, 9, 16, 128), F32),
            pltpu.VMEM((2, 2, 2, 9, 16, 128), F32),
            pltpu.VMEM((7, 32, 128), BF16),
            pltpu.VMEM((7, 32, 128), BF16),
            pltpu.VMEM((2, 16, 128), F32),
            pltpu.VMEM((2, 16, 128), F32),
            pltpu.SemaphoreType.DMA((N_SEMS,)),
            pltpu.SemaphoreType.DMA((N_SEMS,)),
            pltpu.SemaphoreType.DMA((3,)),
        ],
        compiler_params=pltpu.CompilerParams(collective_id=0, has_side_effects=True),
        name="conv_layer",
    )(inputs[0], weights, cotangent[0])
    out, dx, dw = pl.pallas_call(
        place,
        out_shape=(
            jax.ShapeDtypeStruct((8, 32, 128), BF16),
            jax.ShapeDtypeStruct((2, 128, 128), BF16),
            jax.ShapeDtypeStruct((3, 3, 32, 128), F32),
        ),
        in_specs=[vmem] * 3,
        out_specs=[hbm] * 3,
        scratch_shapes=[pltpu.SemaphoreType.DMA((3,))],
        name="place_results",
    )(*(pltpu.with_memory_space_constraint(v, pltpu.VMEM) for v in (out, dx, dw)))
    return out[None], dx[None], dw


def solution(mesh):
    return jax.shard_map(
        body,
        mesh=mesh,
        in_specs=(
            P(None, "filt", None, "chan"),
            P(None, None, "filt", "chan"),
            P(None, "chan", "filt", None),
        ),
        out_specs=(
            P(None, "chan", "filt", None),
            P(None, "filt", None, "chan"),
            P(None, None, "filt", "chan"),
        ),
        check_vma=False,
    )
```

```python
import functools
import math

import jax
import jax.numpy as jnp
from jax import lax
from jax.experimental import pallas as pl
from jax.experimental.pallas import tpu as pltpu
from jax.sharding import PartitionSpec as P

MESH = pl.DeviceIdType.MESH
BF16 = jnp.bfloat16
F32 = jnp.float32

NX, NY, NZ = 4, 4, 8
LANES = 128

PIECES = 4
WAVES = 2


def layout(*sizes):
    return [sum(sizes[:i]) for i in range(len(sizes) + 1)]


Z_RING, X_WAVE, Y_RING = 7 * PIECES, 3 * PIECES // WAVES, 3 * PIECES
R_X, R_W, R_T, R_C, R_DX, R_DW, R_O, R_OC, R_OM, R_OE, R_OH, N_RECV = layout(
    Z_RING, 6, NY, NX, Z_RING, Y_RING, X_WAVE * WAVES, WAVES, WAVES, WAVES, WAVES
)
S_X, S_W, S_T, S_SWAP, S_H, S_C, S_DX, S_DW, S_O, S_OC, S_OM, S_OE, S_OH, N_SEND = layout(*[1] * 13)


def kernel(
    norm,
    x_in, w_in, g_in,
    out_o, dx_o, dw_o,
    out_v, dx_v, dw_v, gin, xg, wg, gg, x3, y3, dyn, wf, wb,
    pdx, rdx, acc, pdw, rdw, po, rk, ro, ob, orx, oe, oh,
    ss, rs, ls, fs,
):
    chan = lax.axis_index("chan")
    filt = lax.axis_index("filt")
    x, k = lax.div(chan, 2), lax.rem(chan, 2)
    y, z = lax.div(filt, NZ), lax.rem(filt, NZ)

    def dev(dx, dk, dy, dz):
        return (dx * 2 + dk, dy * NZ + dz)

    def mod(v, n):
        return lax.rem(v + n, n)

    x_right, x_left = dev(mod(x + 1, NX), k, y, z), dev(mod(x - 1, NX), k, y, z)
    y_right, y_left = dev(x, k, mod(y + 1, NY), z), dev(x, k, mod(y - 1, NY), z)
    z_right, z_left = dev(x, k, y, mod(z + 1, NZ)), dev(x, k, y, mod(z - 1, NZ))
    other = dev(x, 1 - k, y, z)
    swap = dev(y, k, x, z)
    off_diag = x != y
    step = 2 * k - 1
    out_halo_to = dev(mod(y + step, NX), 1 - k, x, z)
    out_halo_from = dev(y, 1 - k, mod(x + step, NY), z)

    loads = [
        pltpu.make_async_copy(g_in, gin, ls.at[0]),
        pltpu.make_async_copy(x_in, xg.at[z], ls.at[1]),
        pltpu.make_async_copy(w_in, wg.at[y], ls.at[2]),
    ]
    for load in loads:
        load.start()

    barrier = pltpu.get_barrier_semaphore()

    def greet(peer):
        pl.semaphore_signal(barrier, inc=1, device_id=peer, device_id_type=MESH)

    for i in range(NY):
        b = mod(y + i, NY)
        greet(dev(mod(y + step, NX), 1 - k, b, z))
        if i:
            greet(dev(y, k, mod(x + i, NY), z))
    for peer in (x_right, x_left, y_right, y_left, z_right, z_left, other, out_halo_from):
        greet(peer)

    @pl.when(off_diag)
    def _():
        greet(swap)

    pdx[...] = jnp.zeros_like(pdx)
    po[...] = jnp.zeros_like(po)
    pl.semaphore_wait(barrier, jnp.where(off_diag, 16, 15))
    for load in loads:
        load.wait()

    def rcopy(src, dst, send, recv, target):
        return pltpu.make_async_remote_copy(
            src_ref=src, dst_ref=dst, send_sem=ss.at[send], recv_sem=rs.at[recv],
            device_id=target, device_id_type=MESH,
        )

    def push(src, dst, send, recv, target):
        rcopy(src, dst, send, recv, target).start()

    def landed(dst, recv):
        rcopy(dst, dst, S_X, recv, other).wait_recv()

    def left_by(size, send):
        rcopy(size, size, send, R_X, other).wait_send()

    def runs(d, pieces, free):
        half = pieces // 2
        first = half if (d == 1) != free else 0
        return range(first, first + half)

    def gather(buf, pos, n, right, left, send_sem, base, cut, pieces):
        last = n // 2

        def piece_at(s, d, piece, hops):
            ref = buf.at[mod(pos - s + hops, n) if d == 0 else mod(pos + s - hops, n)]
            first = runs(d, pieces, False)[0] if s == last else 0
            sem = base + d * (pieces * (last - 1) + pieces // 2) + (s - 1) * pieces + piece - first
            return cut(ref, piece), sem

        def forward(s, free=False):
            for both in zip(runs(0, pieces, free), runs(1, pieces, free)):
                for d in range(2):
                    if s:
                        landed(*piece_at(s, d, both[d], 0))
                    if s + 1 < last or s + 1 == last and not free:
                        ref, recv = piece_at(s + 1, d, both[d], 1)
                        push(ref, ref, send_sem, recv, right if d == 0 else left)

        return forward

    def scatter(part, got, pos, n, right, left, send_sem, base, cut, pieces):
        last = n // 2
        half = pieces // 2

        def dest(t, d):
            away = last + 1 - t
            return mod(pos + away, n) if d == 0 else mod(pos - away, n)

        def sem(t, d, piece):
            first = base + d * (half + pieces * (last - 1))
            if t == 1:
                return first + piece - runs(d, pieces, False)[0]
            return first + half + (t - 2) * pieces + piece

        def each(free):
            for both in zip(runs(0, pieces, free), runs(1, pieces, free)):
                for d in range(2):
                    yield d, both[d]

        def send(t, d, piece):
            push(
                cut(part(dest(t, d)), piece), cut(got.at[d, t - 1], piece), send_sem,
                sem(t, d, piece), right if d == 0 else left,
            )

        def start():
            for d, piece in each(False):
                send(1, d, piece)

        def start_free():
            for d, piece in each(True):
                send(2, d, piece)

        def advance(t, free=False):
            for d, piece in each(free):
                term = cut(got.at[d, t - 1], piece)
                landed(term, sem(t, d, piece))
                cut(part(dest(t + 1, d)), piece)[...] += term[...]
                send(t + 1, d, piece)

        def finish():
            for d in range(2):
                for piece in range(pieces):
                    landed(cut(got.at[d, last - 1], piece), sem(last, d, piece))

        return start, start_free, advance, finish

    def rows_cut(ref, piece):
        return ref.at[piece // 2, pl.ds(64 * (piece % 2), 64)]

    x_forward = gather(xg, z, NZ, z_right, z_left, S_X, R_X, rows_cut, PIECES)
    w_forward = gather(
        wg, y, NY, y_right, y_left, S_W, R_W, lambda ref, i: ref.at[:, :, pl.ds(16 * i, 16)], 2
    )
    dx_start, dx_free, dx_advance, dx_finish = scatter(
        lambda i: pdx.at[i + 1], rdx, z, NZ, z_right, z_left, S_DX, R_DX, rows_cut, PIECES
    )
    dw_start, dw_free, dw_advance, dw_finish = scatter(
        lambda i: pdw.at[i], rdw, y, NY, y_right, y_left, S_DW, R_DW, lambda ref, i: ref.at[i],
        PIECES,
    )
    pk = po.at[k]
    per_wave = PIECES // WAVES
    waves = [
        scatter(
            lambda i: pk.at[i], ro, x, NX, x_right, x_left, S_O, R_O + w * X_WAVE,
            lambda ref, i, first=w * per_wave: ref.at[first + i], per_wave,
        )
        for w in range(WAVES)
    ]

    def main_copy(i):
        return rcopy(
            gin, gg.at[k, y, pl.ds(1 - k, 8)], S_T if i else S_SWAP, R_T + y,
            dev(mod(x + i, NX), k, x, z),
        )

    def self_copy():
        return pltpu.make_async_copy(gin, gg.at[k, y, pl.ds(1 - k, 8)], ls.at[0])

    w_forward(0)
    w_forward(0, free=True)
    for i in (2, 1, 3):
        main_copy(i).start()

    @pl.when(off_diag)
    def _():
        main_copy(0).start()

    @pl.when(jnp.logical_not(off_diag))
    def _():
        self_copy().start()

    for i in range(NX):
        push(
            gin.at[7 * k], gg.at[1 - k, y, 8 * (1 - k)], S_H, R_T + y,
            dev(mod(x + i, NX), 1 - k, mod(x + step, NY), z),
        )

    def cot_block(i):
        b = mod(x + i, NY)
        if i:
            landed(gg.at[k, b], R_T + b)
        else:

            @pl.when(off_diag)
            def _():
                landed(gg.at[k, b], R_T + b)

            @pl.when(jnp.logical_not(off_diag))
            def _():
                landed(gg.at[k, b, 8 * k], R_T + b)
                self_copy().wait()

        push(gg.at[k, b], gg.at[k, b], S_C, R_C + i, other)

    col = lax.broadcasted_iota(jnp.int32, (LANES, LANES), 0)

    def shifts(v):
        before = jnp.where(col == 0, 0.0, pltpu.roll(v, 1, 0))
        after = jnp.where(col == LANES - 1, 0.0, pltpu.roll(v, LANES - 1, 0))
        return before.astype(BF16), after.astype(BF16)

    def y_rows(half):
        def row(ql):
            q = half * 9 + ql
            outside = jnp.logical_or(
                jnp.logical_and(q == 0, y == 0), jnp.logical_and(q == 17, y == NY - 1)
            )
            v = gg[half, :, ql].reshape(LANES, LANES).astype(F32)
            v = jnp.where(outside, 0.0, v)
            at = pl.multiple_of(q * LANES, LANES)
            dyn[:, pl.ds(at, LANES)] = v.astype(BF16)
            t = v.T
            before, after = shifts(t)
            y3[pl.ds(at, LANES), 0:128] = after
            y3[pl.ds(at, LANES), 128:256] = t.astype(BF16)
            y3[pl.ds(at, LANES), 256:384] = before

        def rows(g, carry):
            for u in range(3):
                row(g * 3 + u)
            return carry

        lax.fori_loop(0, 3, rows, 0)

    def x_block(i):
        block = mod(z + i, NZ)
        for u in range(2):
            v16 = xg[block, u]
            before, after = shifts(v16.astype(F32))
            at = pl.multiple_of((block * 2 + u) * LANES, LANES)
            x3[pl.ds(at, LANES), 0:128] = before
            x3[pl.ds(at, LANES), 128:256] = v16
            x3[pl.ds(at, LANES), 256:384] = after

    far = mod(z + NZ // 2, NZ)

    def dx_pair(i):
        t = mod(far + i, 9)
        at = pl.multiple_of(t * 2 * LANES, 2 * LANES)
        r = jnp.dot(y3[pl.ds(at, 2 * LANES), :], wb[...], preferred_element_type=F32)
        r0, r1 = r[:LANES], r[LANES:]
        pdx[t, 0] += r0[:, 0:128]
        pdx[t, 1] += r0[:, 128:256] + r1[:, 0:128]
        pdx[t + 1, 0] += r0[:, 256:384] + r1[:, 128:256]
        pdx[t + 1, 1] += r1[:, 256:384]

    tile = (NX, PIECES, 8, LANES)

    def out_pair(i):
        t = mod(z + i, NZ)
        at = pl.multiple_of(t * 2 * LANES, 2 * LANES)
        r = lax.dot_general(
            wf[...], x3[pl.ds(at, 2 * LANES), :], (((1,), (1,)), ((), ())),
            preferred_element_type=F32,
        )
        r0, r1 = r[:, :LANES], r[:, LANES:]

        def row(q):
            return po.at[lax.div(q, 9), :, :, lax.rem(q, 9)]

        row(2 * t)[...] += r0[256:384].reshape(tile)
        row(2 * t + 1)[...] += (r0[128:256] + r1[256:384]).reshape(tile)
        row(2 * t + 2)[...] += (r0[0:128] + r1[128:256]).reshape(tile)
        row(2 * t + 3)[...] += r1[0:128].reshape(tile)

    def dw_rows(t):
        at = t * 4 * LANES
        lhs = jnp.concatenate(
            [dyn[:, at + (2 - i) * LANES : at + (6 - i) * LANES] for i in range(3)], axis=0
        )
        return jnp.dot(lhs, x3[at : at + 4 * LANES, :], preferred_element_type=F32)

    x_forward(0)
    x_forward(0, free=True)
    x_block(0)
    x_forward(1)
    x_forward(1, free=True)
    x_block(1)
    x_block(-1)
    x_forward(2)
    w_forward(1)
    w_forward(1, free=True)
    x_forward(2, free=True)
    x_block(2)
    x_block(-2)
    for i in (0, 1, 3, 2):
        cot_block(i)
    y_rows(k)
    x_forward(3)
    for i in (0, 1, 3, 2):
        landed(gg.at[1 - k, mod(x + i, NY)], R_C + i)
    y_rows(1 - k)
    w_forward(2)
    for b in range(NY):
        for i in range(3):
            for j in range(3):
                tap = wg[b, i, j]
                wf[i * 128 + b * 32 : i * 128 + b * 32 + 32, j * 128 : j * 128 + 128] = tap
                wb[j * 128 + b * 32 : j * 128 + b * 32 + 32, i * 128 : i * 128 + 128] = tap

    for i in range(2):
        dx_pair(i)
    dx_start()
    for i in (0, 1, -1, 2, -2):
        out_pair(i)
    x_forward(3, free=True)
    for i in (3, -3):
        x_block(i)
        out_pair(i)
    x_forward(4)
    x_block(4)
    out_pair(4)
    for w in range(WAVES):
        mine = pl.ds(w * per_wave, per_wave)
        push(po.at[1 - k, :, mine], rk.at[:, mine], S_OC, R_OC + w, other)
    for i in range(2, 9):
        dx_pair(i)
    dx_free()
    dx_advance(1)

    for w in range(WAVES):
        mine = pl.ds(w * per_wave, per_wave)
        landed(rk.at[:, mine], R_OC + w)
        for i in (2, 1, 3, 0):
            b = mod(x + i, NX)
            pk.at[b, mine][...] += rk[b, w * per_wave : (w + 1) * per_wave]
            if i == 2:
                waves[w][0]()
        waves[w][1]()
    acc[...] = dw_rows(0)
    acc[...] += dw_rows(1)
    acc[...] += dw_rows(2)
    acc[...] += dw_rows(3)
    for b in range(NY):
        for h in range(PIECES):
            for i in range(3):
                at = i * 128 + b * 32 + h * 8
                pdw[b, h, i] = acc[at : at + 8, :]
    dw_start()
    dw_free()
    dx_advance(2, free=True)
    dx_advance(2)
    waves[0][2](1)
    waves[1][2](1)
    dw_advance(1)
    dx_advance(3, free=True)
    dx_advance(3)

    sums = po.at[k, x]

    def out_copies(w):
        edge = sums.at[pl.ds(w * per_wave, per_wave), 7 * k + 1 - k]
        return (ob.at[w], orx.at[w]), (edge, oe.at[w])

    def out_remote(w):
        main, edge = out_copies(w)
        return rcopy(*main, S_OM, R_OM + w, swap), rcopy(*edge, S_OE, R_OE + w, swap)

    def out_local(w):
        main, edge = out_copies(w)
        return (
            pltpu.make_async_copy(*main, ls.at[2 * w]),
            pltpu.make_async_copy(*edge, ls.at[2 * w + 1]),
        )

    def out_wave(w):
        waves[w][3]()
        for h in range(w * per_wave, (w + 1) * per_wave):
            for q in range(9):
                sums[h, q] += ro[0, 1, h, q] + ro[1, 1, h, q]
        push(
            sums.at[pl.ds(w * per_wave, per_wave), 8 * k], oh.at[w], S_OH, R_OH + w, out_halo_to
        )
        for q in range(7):
            pair = sums[w * per_wave : (w + 1) * per_wave, q + 2 * (1 - k)]
            ob[w, q] = pair.reshape(16, LANES).astype(BF16)

        @pl.when(off_diag)
        def _():
            for copy in out_remote(w):
                copy.start()

        @pl.when(jnp.logical_not(off_diag))
        def _():
            for copy in out_local(w):
                copy.start()

    out_wave(0)
    out_wave(1)

    dw_finish()
    for h in range(PIECES):
        for i in range(3):
            total = (pdw[y, h, i] + rdw[0, 1, h, i] + rdw[1, 1, h, i]) * norm
            for j in range(3):
                dw_v[i, j, 8 * h : 8 * h + 8] = total[:, 128 * j : 128 * j + 128]
    stores = [
        pltpu.make_async_copy(dw_v, dw_o, fs.at[0]),
        pltpu.make_async_copy(dx_v, dx_o, fs.at[1]),
        pltpu.make_async_copy(out_v, out_o, fs.at[2]),
    ]
    stores[0].start()

    dx_finish()
    dx_v[...] = (pdx[z + 1] + rdx[0, 3] + rdx[1, 3]).astype(BF16)
    stores[1].start()

    inside = jnp.where(k == 0, x > 0, x < NX - 1)
    for w in range(WAVES):

        @pl.when(off_diag)
        def _():
            for copy in out_remote(w):
                copy.wait_recv()

        @pl.when(jnp.logical_not(off_diag))
        def _():
            for copy in out_local(w):
                copy.wait()

        landed(oh.at[w], R_OH + w)
        out_v[pl.ds(1 - k, 7), 16 * w : 16 * w + 16] = orx[w]
        row = (oe[w] + jnp.where(inside, oh[w], 0.0)).reshape(16, LANES)
        out_v[7 * k, 16 * w : 16 * w + 16] = row.astype(BF16)
    stores[2].start()

    @pl.when(off_diag)
    def _():
        main_copy(0).wait_send()
        left_by(ob, S_OM)
        left_by(oe, S_OE)

    left_by(xg.at[pl.ds(0, 7)], S_X)
    left_by(wg.at[pl.ds(0, 3)], S_W)
    left_by(xg.at[pl.ds(0, 3)], S_T)
    left_by(gin.at[pl.ds(0, 4)], S_H)
    left_by(gg.at[k], S_C)
    left_by(pdx.at[pl.ds(0, 7)], S_DX)
    left_by(pdw.at[pl.ds(0, 3)], S_DW)
    left_by(pk.at[pl.ds(0, 3)], S_O)
    left_by(pk, S_OC)
    left_by(oh, S_OH)
    for store in stores:
        store.wait()


def place(*refs):
    sems = refs[6]
    copies = [pltpu.make_async_copy(refs[i], refs[i + 3], sems.at[i]) for i in range(3)]
    for copy in copies:
        copy.start()
    for copy in copies:
        copy.wait()


def body(inputs, weights, cotangent):
    norm = 1.0 / math.sqrt(inputs.shape[0] * cotangent.shape[1] * 8 * inputs.shape[2])
    vmem = pl.BlockSpec(memory_space=pltpu.VMEM)
    hbm = pl.BlockSpec(memory_space=pl.ANY)
    out, dx, dw = pl.pallas_call(
        functools.partial(kernel, norm),
        out_shape=(
            pltpu.VMEM((8, 32, 128), BF16),
            pltpu.VMEM((2, 128, 128), BF16),
            pltpu.VMEM((3, 3, 32, 128), F32),
        ),
        in_specs=[hbm] * 3,
        out_specs=[hbm] * 3,
        scratch_shapes=[
            pltpu.VMEM((8, 32, 128), BF16),
            pltpu.VMEM((2, 128, 128), BF16),
            pltpu.VMEM((3, 3, 32, 128), F32),
            pltpu.VMEM((8, 32, 128), BF16),
            pltpu.VMEM((8, 2, 128, 128), BF16),
            pltpu.VMEM((4, 3, 3, 32, 128), BF16),
            pltpu.VMEM((2, 4, 9, 32, 128), BF16),
            pltpu.VMEM((2048, 384), BF16),
            pltpu.VMEM((2304, 384), BF16),
            pltpu.VMEM((128, 2304), BF16),
            pltpu.VMEM((384, 384), BF16),
            pltpu.VMEM((384, 384), BF16),
            pltpu.VMEM((10, 2, 128, 128), F32),
            pltpu.VMEM((2, 4, 2, 128, 128), F32),
            pltpu.VMEM((384, 384), F32),
            pltpu.VMEM((4, PIECES, 3, 8, 384), F32),
            pltpu.VMEM((2, 2, PIECES, 3, 8, 384), F32),
            pltpu.VMEM((2, 4, PIECES, 9, 8, 128), F32),
            pltpu.VMEM((4, PIECES, 9, 8, 128), F32),
            pltpu.VMEM((2, 2, PIECES, 9, 8, 128), F32),
            pltpu.VMEM((WAVES, 7, 16, 128), BF16),
            pltpu.VMEM((WAVES, 7, 16, 128), BF16),
            pltpu.VMEM((WAVES, 2, 8, 128), F32),
            pltpu.VMEM((WAVES, 2, 8, 128), F32),
            pltpu.SemaphoreType.DMA((N_SEND,)),
            pltpu.SemaphoreType.DMA((N_RECV,)),
            pltpu.SemaphoreType.DMA((4,)),
            pltpu.SemaphoreType.DMA((3,)),
        ],
        compiler_params=pltpu.CompilerParams(collective_id=0, has_side_effects=True),
        name="conv_layer",
    )(inputs[0], weights, cotangent[0])
    out, dx, dw = pl.pallas_call(
        place,
        out_shape=(
            jax.ShapeDtypeStruct((8, 32, 128), BF16),
            jax.ShapeDtypeStruct((2, 128, 128), BF16),
            jax.ShapeDtypeStruct((3, 3, 32, 128), F32),
        ),
        in_specs=[vmem] * 3,
        out_specs=[hbm] * 3,
        scratch_shapes=[pltpu.SemaphoreType.DMA((3,))],
        name="place_results",
    )(*(pltpu.with_memory_space_constraint(v, pltpu.VMEM) for v in (out, dx, dw)))
    return out[None], dx[None], dw


def solution(mesh):
    return jax.shard_map(
        body,
        mesh=mesh,
        in_specs=(
            P(None, "filt", None, "chan"),
            P(None, None, "filt", "chan"),
            P(None, "chan", "filt", None),
        ),
        out_specs=(
            P(None, "chan", "filt", None),
            P(None, "filt", None, "chan"),
            P(None, None, "filt", "chan"),
        ),
        check_vma=False,
    )
```

```python
import functools
import math

import jax
import jax.numpy as jnp
from jax import lax
from jax.experimental import pallas as pl
from jax.experimental.pallas import tpu as pltpu
from jax.sharding import PartitionSpec as P

MESH = pl.DeviceIdType.MESH
BF16 = jnp.bfloat16
F32 = jnp.float32

NX, NY, NZ = 4, 4, 8
LANES = 128

PIECES = 4
WAVES = 2


def layout(*sizes):
    return [sum(sizes[:i]) for i in range(len(sizes) + 1)]


R_X, R_W, R_T, R_C, R_DX, R_DW, R_O, R_OC, R_OM, R_OE, R_OH, N_RECV = layout(
    12, NY - 1, NY, NX, 2 * (3 * PIECES + PIECES // 2), NY - 1, (NX - 1) * WAVES,
    WAVES, WAVES, WAVES, WAVES,
)
S_X, S_W, S_T, S_SWAP, S_H, S_C, S_DX, S_DW, S_O, S_OC, S_OM, S_OE, S_OH, N_SEND = layout(*[1] * 13)


def kernel(
    norm,
    x_in, w_in, g_in,
    out_o, dx_o, dw_o,
    out_v, dx_v, dw_v, gin, xg, wg, gg, x3, y3, dyn, wf, wb,
    pdx, rdx, acc, pdw, rdw, po, rk, ro, ob, orx, oe, oh,
    ss, rs, ls, fs,
):
    chan = lax.axis_index("chan")
    filt = lax.axis_index("filt")
    x, k = lax.div(chan, 2), lax.rem(chan, 2)
    y, z = lax.div(filt, NZ), lax.rem(filt, NZ)

    def dev(dx, dk, dy, dz):
        return (dx * 2 + dk, dy * NZ + dz)

    def mod(v, n):
        return lax.rem(v + n, n)

    def along_x(i):
        return dev(mod(x + i, NX), k, y, z)

    def along_y(i):
        return dev(x, k, mod(y + i, NY), z)

    def along_z(i):
        return dev(x, k, y, mod(z + i, NZ))

    other = dev(x, 1 - k, y, z)
    off_diag = x != y
    step = 2 * k - 1

    def owner(i, row):
        return lax.rem(2 * row + 2 - i + 2 * NX, NX)

    mine = owner(x, y)
    out_to = dev(y, k, mine, z)
    out_from = dev(owner(y, x), k, x, z)
    above, across = mod(y + step, NX), mod(x + step, NY)
    out_halo_to = dev(above, 1 - k, mine, z)
    out_halo_from = dev(owner(y, across), 1 - k, across, z)

    loads = [
        pltpu.make_async_copy(g_in, gin, ls.at[0]),
        pltpu.make_async_copy(x_in, xg.at[z], ls.at[1]),
        pltpu.make_async_copy(w_in, wg.at[y], ls.at[2]),
    ]
    for load in loads:
        load.start()

    barrier = pltpu.get_barrier_semaphore()

    def greet(peer):
        pl.semaphore_signal(barrier, inc=1, device_id=peer, device_id_type=MESH)

    for i in range(NY):
        b = mod(y + i, NY)
        greet(dev(mod(y + step, NX), 1 - k, b, z))
        if i:
            greet(dev(y, k, mod(x + i, NY), z))
    for peer in (
        *[along_x(i) for i in (1, 2, 3)], *[along_y(i) for i in (1, 2, 3)],
        *[along_z(i) for i in (-2, -1, 1, 2)], other, out_from, out_halo_from,
    ):
        greet(peer)

    @pl.when(off_diag)
    def _():
        greet(dev(y, k, x, z))

    pl.semaphore_wait(barrier, jnp.where(off_diag, 21, 20))
    for load in loads:
        load.wait()

    def rcopy(src, dst, send, recv, target):
        return pltpu.make_async_remote_copy(
            src_ref=src, dst_ref=dst, send_sem=ss.at[send], recv_sem=rs.at[recv],
            device_id=target, device_id_type=MESH,
        )

    def push(src, dst, send, recv, target):
        rcopy(src, dst, send, recv, target).start()

    def landed(dst, recv):
        rcopy(dst, dst, S_X, recv, other).wait_recv()

    def left_by(size, send):
        rcopy(size, size, send, R_X, other).wait_send()

    ways = (1, -1)

    def x_send(d, away, reach, row, slot):
        ref = xg.at[mod(z - ways[d] * away, NZ), row]
        push(ref, ref, S_X, R_X + 6 * d + slot, along_z(ways[d] * reach))

    def x_landed(d, away, row, slot):
        landed(xg.at[mod(z - ways[d] * away, NZ), row], R_X + 6 * d + slot)

    def x_start():
        for turn in range(2):
            for d in range(2):
                x_send(d, 0, 2, d if turn == 0 else 1 - d, turn)
        for d in range(2):
            block = xg.at[z]
            push(block, block, S_X, R_X + 6 * d + 2, along_z(ways[d]))

    def x_relay():
        for turn in range(2):
            for d in range(2):
                row = d if turn == 0 else 1 - d
                x_landed(d, 2, row, turn)
                if turn == 0:
                    x_send(d, 2, 2, row, 3)
                x_send(d, 2, 1, row, 4 + turn)

    def x_near():
        for d in range(2):
            landed(xg.at[mod(z - ways[d], NZ)], R_X + 6 * d + 2)

    def x_third():
        for turn in range(2):
            for d in range(2):
                x_landed(d, 3, d if turn == 0 else 1 - d, 4 + turn)

    def x_fourth():
        for d in range(2):
            x_landed(d, 4, d, 3)

    half = PIECES // 2
    far_pieces = (range(half), range(half, PIECES))

    def dx_cut(ref, piece):
        return ref.at[piece // 2, pl.ds(64 * (piece % 2), 64)]

    def dx_sem(d, stage, piece):
        return R_DX + d * (3 * PIECES + half) + (piece - d * half if stage == 0 else half + (stage - 1) * PIECES + piece)

    def dx_send(d, away, reach, stage, piece):
        push(
            dx_cut(pdx.at[mod(z + ways[d] * away, NZ) + 1], piece),
            dx_cut(rdx.at[d, stage], piece), S_DX, dx_sem(d, stage, piece),
            along_z(ways[d] * reach),
        )

    def dx_order(d):
        return (*far_pieces[1 - d], *far_pieces[d])

    def dx_fourth():
        for i in range(half):
            for d in range(2):
                dx_send(d, 4, 2, 0, far_pieces[d][i])

    def dx_third():
        for i in range(PIECES):
            for d in range(2):
                dx_send(d, 3, 1, 1, dx_order(d)[i])

    def dx_add(d, away, stage, piece):
        term = dx_cut(rdx.at[d, stage], piece)
        landed(term, dx_sem(d, stage, piece))
        dx_cut(pdx.at[mod(z + ways[d] * away, NZ) + 1], piece)[...] += term[...]

    def dx_second(far):
        for i in range(half):
            for d in range(2):
                piece = far_pieces[d if far else 1 - d][i]
                dx_add(d, 2, 1, piece)
                if far:
                    dx_add(d, 2, 0, piece)
                dx_send(d, 2, 1, 2, piece)

    def dx_first(far):
        for i in range(half):
            for d in range(2):
                piece = far_pieces[d if far else 1 - d][i]
                dx_add(d, 1, 2, piece)
                dx_send(d, 1, 1, 3, piece)

    def dx_finish():
        for d in range(2):
            for piece in range(PIECES):
                landed(dx_cut(rdx.at[d, 3], piece), dx_sem(d, 3, piece))

    pk = po.at[k]
    per_wave = PIECES // WAVES
    offsets = (2, 1, 3)

    def o_part(w, i):
        return pk.at[owner(mod(x + i, NX), y), pl.ds(w * per_wave, per_wave)]

    def o_slot(w, i):
        return ro.at[i - 1, pl.ds(w * per_wave, per_wave)], R_O + w * (NX - 1) + i - 1

    def o_send(w, i):
        dst, recv = o_slot(w, i)
        push(o_part(w, i), dst, S_O, recv, along_x(i))

    def main_copy(i):
        return rcopy(
            gin, gg.at[k, y, pl.ds(1 - k, 8)], S_T if i else S_SWAP, R_T + y,
            dev(mod(x + i, NX), k, x, z),
        )

    def self_copy():
        return pltpu.make_async_copy(gin, gg.at[k, y, pl.ds(1 - k, 8)], ls.at[0])

    for i in (2, 1, 3):
        main_copy(i).start()

    @pl.when(off_diag)
    def _():
        main_copy(0).start()

    @pl.when(jnp.logical_not(off_diag))
    def _():
        self_copy().start()

    for i in range(NX):
        push(
            gin.at[7 * k], gg.at[1 - k, y, 8 * (1 - k)], S_H, R_T + y,
            dev(mod(x + i, NX), 1 - k, mod(x + step, NY), z),
        )
    for i in offsets:
        push(wg.at[y], wg.at[y], S_W, R_W + i - 1, along_y(i))

    def cot_block(i):
        b = mod(x + i, NY)
        if i:
            landed(gg.at[k, b], R_T + b)
        else:

            @pl.when(off_diag)
            def _():
                landed(gg.at[k, b], R_T + b)

            @pl.when(jnp.logical_not(off_diag))
            def _():
                landed(gg.at[k, b, 8 * k], R_T + b)
                self_copy().wait()

        push(gg.at[k, b], gg.at[k, b], S_C, R_C + i, other)

    col = lax.broadcasted_iota(jnp.int32, (LANES, LANES), 0)

    def shifts(v):
        before = jnp.where(col == 0, 0.0, pltpu.roll(v, 1, 0))
        after = jnp.where(col == LANES - 1, 0.0, pltpu.roll(v, LANES - 1, 0))
        return before.astype(BF16), after.astype(BF16)

    def y_rows(half):
        def row(ql):
            q = half * 9 + ql
            outside = jnp.logical_or(
                jnp.logical_and(q == 0, y == 0), jnp.logical_and(q == 17, y == NY - 1)
            )
            v = gg[half, :, ql].reshape(LANES, LANES).astype(F32)
            v = jnp.where(outside, 0.0, v)
            at = pl.multiple_of(q * LANES, LANES)
            dyn[:, pl.ds(at, LANES)] = v.astype(BF16)
            t = v.T
            before, after = shifts(t)
            y3[pl.ds(at, LANES), 0:128] = after
            y3[pl.ds(at, LANES), 128:256] = t.astype(BF16)
            y3[pl.ds(at, LANES), 256:384] = before

        def rows(g, carry):
            for u in range(3):
                row(g * 3 + u)
            return carry

        lax.fori_loop(0, 3, rows, 0)

    def x_block(i):
        block = mod(z + i, NZ)
        for u in range(2):
            v16 = xg[block, u]
            before, after = shifts(v16.astype(F32))
            at = pl.multiple_of((block * 2 + u) * LANES, LANES)
            x3[pl.ds(at, LANES), 0:128] = before
            x3[pl.ds(at, LANES), 128:256] = v16
            x3[pl.ds(at, LANES), 256:384] = after

    far = mod(z + NZ // 2, NZ)

    def dx_pair(i):
        t = mod(far + i, 9)
        at = pl.multiple_of(t * 2 * LANES, 2 * LANES)
        r = jnp.dot(y3[pl.ds(at, 2 * LANES), :], wb[...], preferred_element_type=F32)
        r0, r1 = r[:LANES], r[LANES:]
        pdx[t, 0] += r0[:, 0:128]
        pdx[t, 1] += r0[:, 128:256] + r1[:, 0:128]
        pdx[t + 1, 0] += r0[:, 256:384] + r1[:, 128:256]
        pdx[t + 1, 1] += r1[:, 256:384]

    tile = (NX, PIECES, 8, LANES)

    def out_pair(i):
        t = (1 - k) * 7 + step * i
        at = pl.multiple_of(t * 2 * LANES, 2 * LANES)
        r = lax.dot_general(
            wf[...], x3[pl.ds(at, 2 * LANES), :], (((1,), (1,)), ((), ())),
            preferred_element_type=F32,
        )
        r0, r1 = r[:, :LANES], r[:, LANES:]

        def row(q):
            return po.at[lax.div(q, 9), :, :, lax.rem(q, 9)]

        row(2 * t)[...] += r0[256:384].reshape(tile)
        row(2 * t + 1)[...] += (r0[128:256] + r1[256:384]).reshape(tile)
        row(2 * t + 2)[...] += (r0[0:128] + r1[128:256]).reshape(tile)
        row(2 * t + 3)[...] += r1[0:128].reshape(tile)

    def dw_rows(t):
        at = t * 4 * LANES
        lhs = jnp.concatenate(
            [dyn[:, at + (2 - i) * LANES : at + (6 - i) * LANES] for i in range(3)], axis=0
        )
        return jnp.dot(lhs, x3[at : at + 4 * LANES, :], preferred_element_type=F32)

    x_start()
    pdx[...] = jnp.zeros_like(pdx)
    po[...] = jnp.zeros_like(po)
    x_block(0)
    x_relay()
    for i in (0, 1, 3, 2):
        cot_block(i)
    x_near()
    for i in (1, -1, 2, -2):
        x_block(i)
    y_rows(k)
    for i in (0, 1, 3, 2):
        landed(gg.at[1 - k, mod(x + i, NY)], R_C + i)
    y_rows(1 - k)
    for i in offsets:
        landed(wg.at[mod(y - i, NY)], R_W + i - 1)
    for b in range(NY):
        for i in range(3):
            for j in range(3):
                tap = wg[b, i, j]
                wf[i * 128 + b * 32 : i * 128 + b * 32 + 32, j * 128 : j * 128 + 128] = tap
                wb[j * 128 + b * 32 : j * 128 + b * 32 + 32, i * 128 : i * 128 + 128] = tap

    for i in range(2):
        dx_pair(i)
    dx_fourth()
    x_third()
    for i in (3, -3):
        x_block(i)
    x_fourth()
    x_block(4)
    for i in range(5):
        out_pair(i)
    for w in range(WAVES):
        part = pl.ds(w * per_wave, per_wave)
        push(po.at[1 - k, :, part], rk.at[:, part], S_OC, R_OC + w, other)
    for i in range(5, 8):
        out_pair(i)
    for i in (2, 3, 7, 8):
        dx_pair(i)
    dx_third()
    for w in range(WAVES):
        part = pl.ds(w * per_wave, per_wave)
        landed(rk.at[:, part], R_OC + w)
        for i in (*offsets, 0):
            b = owner(mod(x + i, NX), y)
            pk.at[b, part][...] += rk[b, w * per_wave : (w + 1) * per_wave]
            if i:
                o_send(w, i)
    for i in (4, 5, 6):
        dx_pair(i)
    acc[...] = dw_rows(0)
    acc[...] += dw_rows(1)
    acc[...] += dw_rows(2)
    acc[...] += dw_rows(3)
    for b in range(NY):
        for h in range(PIECES):
            for i in range(3):
                at = i * 128 + b * 32 + h * 8
                pdw[b, h, i] = acc[at : at + 8, :]
    for i in offsets:
        push(pdw.at[mod(y + i, NY)], rdw.at[i - 1], S_DW, R_DW + i - 1, along_y(i))
    dx_second(False)
    dx_second(True)
    dx_first(False)

    sums = po.at[k, mine]

    def out_copies(w):
        part = pl.ds(w * per_wave, per_wave)
        return (
            rcopy(ob.at[w], orx.at[w], S_OM, R_OM + w, out_to),
            rcopy(sums.at[part, 7 * k + 1 - k], oe.at[w], S_OE, R_OE + w, out_to),
            rcopy(sums.at[part, 8 * k], oh.at[w], S_OH, R_OH + w, out_halo_to),
        )

    def out_wave(w):
        for i in offsets:
            landed(*o_slot(w, i))
        for h in range(w * per_wave, (w + 1) * per_wave):
            for q in range(9):
                sums[h, q] += ro[0, h, q] + ro[1, h, q] + ro[2, h, q]
        main, edge, halo = out_copies(w)
        halo.start()
        edge.start()
        for q in range(7):
            pair = sums[w * per_wave : (w + 1) * per_wave, q + 2 * (1 - k)]
            ob[w, q] = pair.reshape(16, LANES).astype(BF16)
        main.start()

    out_wave(0)
    dx_first(True)
    out_wave(1)

    for i in offsets:
        landed(rdw.at[i - 1], R_DW + i - 1)
    for h in range(PIECES):
        for i in range(3):
            total = (pdw[y, h, i] + rdw[0, h, i] + rdw[1, h, i] + rdw[2, h, i]) * norm
            for j in range(3):
                dw_v[i, j, 8 * h : 8 * h + 8] = total[:, 128 * j : 128 * j + 128]
    stores = [
        pltpu.make_async_copy(dw_v, dw_o, fs.at[0]),
        pltpu.make_async_copy(dx_v, dx_o, fs.at[1]),
        pltpu.make_async_copy(out_v, out_o, fs.at[2]),
    ]
    stores[0].start()

    dx_finish()
    dx_v[...] = (pdx[z + 1] + rdx[0, 3] + rdx[1, 3]).astype(BF16)
    stores[1].start()

    inside = jnp.where(k == 0, x > 0, x < NX - 1)
    for w in range(WAVES):
        for copy in out_copies(w):
            copy.wait_recv()
        out_v[pl.ds(1 - k, 7), 16 * w : 16 * w + 16] = orx[w]
        row = (oe[w] + jnp.where(inside, oh[w], 0.0)).reshape(16, LANES)
        out_v[7 * k, 16 * w : 16 * w + 16] = row.astype(BF16)
    stores[2].start()

    @pl.when(off_diag)
    def _():
        main_copy(0).wait_send()

    left_by(ob, S_OM)
    left_by(oe, S_OE)
    left_by(xg.at[pl.ds(0, 7)], S_X)
    left_by(wg.at[pl.ds(0, 3)], S_W)
    left_by(xg.at[pl.ds(0, 3)], S_T)
    left_by(gin.at[pl.ds(0, 4)], S_H)
    left_by(gg.at[k], S_C)
    left_by(pdx.at[pl.ds(0, 7)], S_DX)
    left_by(pdw.at[pl.ds(0, 3)], S_DW)
    left_by(pk.at[pl.ds(0, 3)], S_O)
    left_by(pk, S_OC)
    left_by(oh, S_OH)
    for store in stores:
        store.wait()


def place(*refs):
    sems = refs[6]
    copies = [pltpu.make_async_copy(refs[i], refs[i + 3], sems.at[i]) for i in range(3)]
    for copy in copies:
        copy.start()
    for copy in copies:
        copy.wait()


def body(inputs, weights, cotangent):
    norm = 1.0 / math.sqrt(inputs.shape[0] * cotangent.shape[1] * 8 * inputs.shape[2])
    vmem = pl.BlockSpec(memory_space=pltpu.VMEM)
    hbm = pl.BlockSpec(memory_space=pl.ANY)
    out, dx, dw = pl.pallas_call(
        functools.partial(kernel, norm),
        out_shape=(
            pltpu.VMEM((8, 32, 128), BF16),
            pltpu.VMEM((2, 128, 128), BF16),
            pltpu.VMEM((3, 3, 32, 128), F32),
        ),
        in_specs=[hbm] * 3,
        out_specs=[hbm] * 3,
        scratch_shapes=[
            pltpu.VMEM((8, 32, 128), BF16),
            pltpu.VMEM((2, 128, 128), BF16),
            pltpu.VMEM((3, 3, 32, 128), F32),
            pltpu.VMEM((8, 32, 128), BF16),
            pltpu.VMEM((8, 2, 128, 128), BF16),
            pltpu.VMEM((4, 3, 3, 32, 128), BF16),
            pltpu.VMEM((2, 4, 9, 32, 128), BF16),
            pltpu.VMEM((2048, 384), BF16),
            pltpu.VMEM((2304, 384), BF16),
            pltpu.VMEM((128, 2304), BF16),
            pltpu.VMEM((384, 384), BF16),
            pltpu.VMEM((384, 384), BF16),
            pltpu.VMEM((10, 2, 128, 128), F32),
            pltpu.VMEM((2, 4, 2, 128, 128), F32),
            pltpu.VMEM((384, 384), F32),
            pltpu.VMEM((4, PIECES, 3, 8, 384), F32),
            pltpu.VMEM((3, PIECES, 3, 8, 384), F32),
            pltpu.VMEM((2, 4, PIECES, 9, 8, 128), F32),
            pltpu.VMEM((4, PIECES, 9, 8, 128), F32),
            pltpu.VMEM((3, PIECES, 9, 8, 128), F32),
            pltpu.VMEM((WAVES, 7, 16, 128), BF16),
            pltpu.VMEM((WAVES, 7, 16, 128), BF16),
            pltpu.VMEM((WAVES, 2, 8, 128), F32),
            pltpu.VMEM((WAVES, 2, 8, 128), F32),
            pltpu.SemaphoreType.DMA((N_SEND,)),
            pltpu.SemaphoreType.DMA((N_RECV,)),
            pltpu.SemaphoreType.DMA((3,)),
            pltpu.SemaphoreType.DMA((3,)),
        ],
        compiler_params=pltpu.CompilerParams(collective_id=0, has_side_effects=True),
        name="conv_layer",
    )(inputs[0], weights, cotangent[0])
    out, dx, dw = pl.pallas_call(
        place,
        out_shape=(
            jax.ShapeDtypeStruct((8, 32, 128), BF16),
            jax.ShapeDtypeStruct((2, 128, 128), BF16),
            jax.ShapeDtypeStruct((3, 3, 32, 128), F32),
        ),
        in_specs=[vmem] * 3,
        out_specs=[hbm] * 3,
        scratch_shapes=[pltpu.SemaphoreType.DMA((3,))],
        name="place_results",
    )(*(pltpu.with_memory_space_constraint(v, pltpu.VMEM) for v in (out, dx, dw)))
    return out[None], dx[None], dw


def solution(mesh):
    return jax.shard_map(
        body,
        mesh=mesh,
        in_specs=(
            P(None, "filt", None, "chan"),
            P(None, None, "filt", "chan"),
            P(None, "chan", "filt", None),
        ),
        out_specs=(
            P(None, "chan", "filt", None),
            P(None, "filt", None, "chan"),
            P(None, None, "filt", "chan"),
        ),
        check_vma=False,
    )
```

```python
import functools
import math

import jax
import jax.numpy as jnp
from jax import lax
from jax.experimental import pallas as pl
from jax.experimental.pallas import tpu as pltpu
from jax.sharding import PartitionSpec as P

MESH = pl.DeviceIdType.MESH
BF16 = jnp.bfloat16
F32 = jnp.float32

NX, NY, NZ = 4, 4, 8
LANES = 128

PIECES = 4
WAVES = 2


def layout(*sizes):
    return [sum(sizes[:i]) for i in range(len(sizes) + 1)]


R_X, R_W, R_T, R_C, R_DX, R_DW, R_O, R_OC, R_OM, R_OE, R_OH, N_RECV = layout(
    12, NY - 1, NY, NX, 2 * (3 * PIECES + PIECES // 2), NY - 1, (NX - 1) * WAVES,
    WAVES, WAVES, WAVES, WAVES,
)
S_X, S_W, S_T, S_SWAP, S_H, S_C, S_DX, S_DW, S_O, S_OC, S_OM, S_OE, S_OH, N_SEND = layout(*[1] * 13)


def kernel(
    norm,
    x_in, w_in, g_in,
    out_o, dx_o, dw_o,
    out_v, dx_v, dw_v, gin, xg, wg, gg, x3, y3, dyn, wf, wb,
    pdx, rdx, acc, pdw, rdw, po, rk, ro, ob, orx, oe, oh,
    ss, rs, ls, fs,
):
    chan = lax.axis_index("chan")
    filt = lax.axis_index("filt")
    x, k = lax.div(chan, 2), lax.rem(chan, 2)
    y, z = lax.div(filt, NZ), lax.rem(filt, NZ)

    def dev(dx, dk, dy, dz):
        return (dx * 2 + dk, dy * NZ + dz)

    def mod(v, n):
        return lax.rem(v + n, n)

    def along_x(i):
        return dev(mod(x + i, NX), k, y, z)

    def along_y(i):
        return dev(x, k, mod(y + i, NY), z)

    def along_z(i):
        return dev(x, k, y, mod(z + i, NZ))

    other = dev(x, 1 - k, y, z)
    off_diag = x != y
    step = 2 * k - 1

    def owner(i, row):
        return lax.rem(2 * row + 2 - i + 2 * NX, NX)

    mine = owner(x, y)
    out_to = dev(y, k, mine, z)
    out_from = dev(owner(y, x), k, x, z)
    above, across = mod(y + step, NX), mod(x + step, NY)
    out_halo_to = dev(above, 1 - k, mine, z)
    out_halo_from = dev(owner(y, across), 1 - k, across, z)

    loads = [
        pltpu.make_async_copy(g_in, gin, ls.at[0]),
        pltpu.make_async_copy(x_in, xg.at[z], ls.at[1]),
        pltpu.make_async_copy(w_in, wg.at[y], ls.at[2]),
    ]
    for load in loads:
        load.start()

    barrier = pltpu.get_barrier_semaphore()

    def greet(peer):
        pl.semaphore_signal(barrier, inc=1, device_id=peer, device_id_type=MESH)

    for i in range(NY):
        b = mod(y + i, NY)
        greet(dev(mod(y + step, NX), 1 - k, b, z))
        if i:
            greet(dev(y, k, mod(x + i, NY), z))
    for peer in (
        *[along_x(i) for i in (1, 2, 3)], *[along_y(i) for i in (1, 2, 3)],
        *[along_z(i) for i in (-2, -1, 1, 2)], other, out_from, out_halo_from,
    ):
        greet(peer)

    @pl.when(off_diag)
    def _():
        greet(dev(y, k, x, z))

    pl.semaphore_wait(barrier, jnp.where(off_diag, 21, 20))
    for load in loads:
        load.wait()

    def rcopy(src, dst, send, recv, target):
        return pltpu.make_async_remote_copy(
            src_ref=src, dst_ref=dst, send_sem=ss.at[send], recv_sem=rs.at[recv],
            device_id=target, device_id_type=MESH,
        )

    def push(src, dst, send, recv, target):
        rcopy(src, dst, send, recv, target).start()

    def landed(dst, recv):
        rcopy(dst, dst, S_X, recv, other).wait_recv()

    def left_by(size, send):
        rcopy(size, size, send, R_X, other).wait_send()

    ways = (1, -1)

    def x_send(d, away, reach, row, slot):
        ref = xg.at[mod(z - ways[d] * away, NZ), row]
        push(ref, ref, S_X, R_X + 6 * d + slot, along_z(ways[d] * reach))

    def x_landed(d, away, row, slot):
        landed(xg.at[mod(z - ways[d] * away, NZ), row], R_X + 6 * d + slot)

    def x_start():
        for turn in range(2):
            for d in range(2):
                x_send(d, 0, 2, d if turn == 0 else 1 - d, turn)
        for d in range(2):
            block = xg.at[z]
            push(block, block, S_X, R_X + 6 * d + 2, along_z(ways[d]))

    def x_relay():
        for turn in range(2):
            for d in range(2):
                row = d if turn == 0 else 1 - d
                x_landed(d, 2, row, turn)
                if turn == 0:
                    x_send(d, 2, 2, row, 3)
                x_send(d, 2, 1, row, 4 + turn)

    def x_near():
        for d in range(2):
            landed(xg.at[mod(z - ways[d], NZ)], R_X + 6 * d + 2)

    def x_third():
        for turn in range(2):
            for d in range(2):
                x_landed(d, 3, d if turn == 0 else 1 - d, 4 + turn)

    def x_fourth():
        for d in range(2):
            x_landed(d, 4, d, 3)

    half = PIECES // 2
    far_pieces = (range(half), range(half, PIECES))

    def dx_cut(ref, piece):
        return ref.at[piece // 2, pl.ds(64 * (piece % 2), 64)]

    def dx_sem(d, stage, piece):
        return R_DX + d * (3 * PIECES + half) + (piece - d * half if stage == 0 else half + (stage - 1) * PIECES + piece)

    def dx_send(d, away, reach, stage, piece):
        push(
            dx_cut(pdx.at[mod(z + ways[d] * away, NZ) + 1], piece),
            dx_cut(rdx.at[d, stage], piece), S_DX, dx_sem(d, stage, piece),
            along_z(ways[d] * reach),
        )

    def dx_order(d):
        return (*far_pieces[d], *far_pieces[1 - d])

    def dx_fourth():
        for i in range(half):
            for d in range(2):
                dx_send(d, 4, 2, 0, far_pieces[d][i])

    def dx_third():
        for i in range(PIECES):
            for d in range(2):
                dx_send(d, 3, 1, 1, dx_order(d)[i])

    def dx_add(d, away, stage, piece):
        term = dx_cut(rdx.at[d, stage], piece)
        landed(term, dx_sem(d, stage, piece))
        dx_cut(pdx.at[mod(z + ways[d] * away, NZ) + 1], piece)[...] += term[...]

    def dx_second(far):
        for i in range(half):
            for d in range(2):
                piece = far_pieces[d if far else 1 - d][i]
                dx_add(d, 2, 1, piece)
                if far:
                    dx_add(d, 2, 0, piece)
                dx_send(d, 2, 1, 2, piece)

    def dx_first(far):
        for i in range(half):
            for d in range(2):
                piece = far_pieces[d if far else 1 - d][i]
                dx_add(d, 1, 2, piece)
                dx_send(d, 1, 1, 3, piece)

    def dx_finish():
        for d in range(2):
            for piece in range(PIECES):
                landed(dx_cut(rdx.at[d, 3], piece), dx_sem(d, 3, piece))

    pk = po.at[k]
    per_wave = PIECES // WAVES
    offsets = (2, 1, 3)

    def o_part(w, i):
        return pk.at[owner(mod(x + i, NX), y), pl.ds(w * per_wave, per_wave)]

    def o_slot(w, i):
        return ro.at[i - 1, pl.ds(w * per_wave, per_wave)], R_O + w * (NX - 1) + i - 1

    def o_send(w, i):
        dst, recv = o_slot(w, i)
        push(o_part(w, i), dst, S_O, recv, along_x(i))

    def main_copy(i):
        return rcopy(
            gin, gg.at[k, y, pl.ds(1 - k, 8)], S_T if i else S_SWAP, R_T + y,
            dev(mod(x + i, NX), k, x, z),
        )

    def self_copy():
        return pltpu.make_async_copy(gin, gg.at[k, y, pl.ds(1 - k, 8)], ls.at[0])

    for i in (2, 1, 3):
        main_copy(i).start()

    @pl.when(off_diag)
    def _():
        main_copy(0).start()

    @pl.when(jnp.logical_not(off_diag))
    def _():
        self_copy().start()

    for i in range(NX):
        push(
            gin.at[7 * k], gg.at[1 - k, y, 8 * (1 - k)], S_H, R_T + y,
            dev(mod(x + i, NX), 1 - k, mod(x + step, NY), z),
        )
    for i in offsets:
        push(wg.at[y], wg.at[y], S_W, R_W + i - 1, along_y(i))

    def cot_block(i):
        b = mod(x + i, NY)
        if i:
            landed(gg.at[k, b], R_T + b)
        else:

            @pl.when(off_diag)
            def _():
                landed(gg.at[k, b], R_T + b)

            @pl.when(jnp.logical_not(off_diag))
            def _():
                landed(gg.at[k, b, 8 * k], R_T + b)
                self_copy().wait()

        push(gg.at[k, b], gg.at[k, b], S_C, R_C + i, other)

    col = lax.broadcasted_iota(jnp.int32, (LANES, LANES), 0)

    def shifts(v):
        before = jnp.where(col == 0, 0.0, pltpu.roll(v, 1, 0))
        after = jnp.where(col == LANES - 1, 0.0, pltpu.roll(v, LANES - 1, 0))
        return before.astype(BF16), after.astype(BF16)

    def y_rows(half):
        def row(ql):
            q = half * 9 + ql
            outside = jnp.logical_or(
                jnp.logical_and(q == 0, y == 0), jnp.logical_and(q == 17, y == NY - 1)
            )
            v = gg[half, :, ql].reshape(LANES, LANES).astype(F32)
            v = jnp.where(outside, 0.0, v)
            at = pl.multiple_of(q * LANES, LANES)
            dyn[:, pl.ds(at, LANES)] = v.astype(BF16)
            t = v.T
            before, after = shifts(t)
            y3[pl.ds(at, LANES), 0:128] = after
            y3[pl.ds(at, LANES), 128:256] = t.astype(BF16)
            y3[pl.ds(at, LANES), 256:384] = before

        for ql in range(9):
            row(ql)

    def x_block(i):
        block = mod(z + i, NZ)
        for u in range(2):
            v16 = xg[block, u]
            before, after = shifts(v16.astype(F32))
            at = pl.multiple_of((block * 2 + u) * LANES, LANES)
            x3[pl.ds(at, LANES), 0:128] = before
            x3[pl.ds(at, LANES), 128:256] = v16
            x3[pl.ds(at, LANES), 256:384] = after

    far = mod(z + NZ // 2, NZ)

    def dx_pair(i):
        t = mod(far + i, 9)
        at = pl.multiple_of(t * 2 * LANES, 2 * LANES)
        r = jnp.dot(y3[pl.ds(at, 2 * LANES), :], wb[...], preferred_element_type=F32)
        r0, r1 = r[:LANES], r[LANES:]
        pdx[t, 0] += r0[:, 0:128]
        pdx[t, 1] += r0[:, 128:256] + r1[:, 0:128]
        pdx[t + 1, 0] += r0[:, 256:384] + r1[:, 128:256]
        pdx[t + 1, 1] += r1[:, 256:384]

    tile = (NX, PIECES // WAVES, 8, LANES)

    def out_pair(i, w):
        t = (1 - k) * 7 + step * i
        at = pl.multiple_of(t * 2 * LANES, 2 * LANES)
        r = lax.dot_general(
            wf[192 * w : 192 * w + 192], x3[pl.ds(at, 2 * LANES), :], (((1,), (1,)), ((), ())),
            preferred_element_type=F32,
        )
        r0, r1 = r[:, :LANES], r[:, LANES:]

        def row(q):
            return po.at[lax.div(q, 9), :, pl.ds(w * per_wave, per_wave), lax.rem(q, 9)]

        row(2 * t)[...] += r0[128:192].reshape(tile)
        row(2 * t + 1)[...] += (r0[64:128] + r1[128:192]).reshape(tile)
        row(2 * t + 2)[...] += (r0[0:64] + r1[64:128]).reshape(tile)
        row(2 * t + 3)[...] += r1[0:64].reshape(tile)

    def dw_all():
        lhs = jnp.concatenate(
            [dyn[:, (2 - i) * LANES : (18 - i) * LANES] for i in range(3)], axis=0
        )
        acc[...] = jnp.dot(lhs, x3[...], preferred_element_type=F32)
        for b in range(NY):
            for i in range(3):
                pdw[b, i] = acc[128 * i + 32 * b : 128 * i + 32 * b + 32, :]
        for away in offsets:
            push(
                pdw.at[mod(y + away, NY)], rdw.at[away - 1], S_DW, R_DW + away - 1, along_y(away)
            )

    x_start()
    pdx[...] = jnp.zeros_like(pdx)
    po[...] = jnp.zeros_like(po)
    x_block(0)
    x_relay()
    for i in (0, 1, 3, 2):
        cot_block(i)
    x_near()
    for i in (1, -1, 2, -2):
        x_block(i)
    y_rows(k)
    for i in (0, 1, 3, 2):
        landed(gg.at[1 - k, mod(x + i, NY)], R_C + i)
    y_rows(1 - k)
    for i in offsets:
        landed(wg.at[mod(y - i, NY)], R_W + i - 1)
    for b in range(NY):
        for i in range(3):
            for j in range(3):
                tap = wg[b, i, j]
                for w in range(WAVES):
                    at = w * 192 + i * 64 + b * 16
                    wf[at : at + 16, j * 128 : j * 128 + 128] = tap[16 * w : 16 * w + 16]
                wb[j * 128 + b * 32 : j * 128 + b * 32 + 32, i * 128 : i * 128 + 128] = tap

    for i in (0, 1):
        dx_pair(i)
    dx_fourth()
    for i in (2, 3, 7, 8):
        dx_pair(i)
    dx_third()
    x_third()
    for i in (3, -3):
        x_block(i)
    x_fourth()
    x_block(4)
    for w in range(WAVES):
        for i in range(5):
            out_pair(i, w)
        part = pl.ds(w * per_wave, per_wave)
        push(po.at[1 - k, :, part], rk.at[:, part], S_OC, R_OC + w, other)
    for w in range(WAVES):
        for i in range(5, 8):
            out_pair(i, w)
    def core_sum(w):
        part = pl.ds(w * per_wave, per_wave)
        landed(rk.at[:, part], R_OC + w)
        for i in (*offsets, 0):
            b = owner(mod(x + i, NX), y)
            pk.at[b, part][...] += rk[b, w * per_wave : (w + 1) * per_wave]
            if i:
                o_send(w, i)

    core_sum(0)
    for i in (4, 5, 6):
        dx_pair(i)
    core_sum(1)
    dw_all()
    dx_second(True)
    dx_second(False)

    sums = po.at[k, mine]

    def out_copies(w):
        part = pl.ds(w * per_wave, per_wave)
        return (
            rcopy(ob.at[w], orx.at[w], S_OM, R_OM + w, out_to),
            rcopy(sums.at[part, 7 * k + 1 - k], oe.at[w], S_OE, R_OE + w, out_to),
            rcopy(sums.at[part, 8 * k], oh.at[w], S_OH, R_OH + w, out_halo_to),
        )

    def out_wave(w):
        for i in offsets:
            landed(*o_slot(w, i))
        for h in range(w * per_wave, (w + 1) * per_wave):
            for q in range(9):
                sums[h, q] += ro[0, h, q] + ro[1, h, q] + ro[2, h, q]
        main, edge, halo = out_copies(w)
        halo.start()
        edge.start()
        for q in range(7):
            pair = sums[w * per_wave : (w + 1) * per_wave, q + 2 * (1 - k)]
            ob[w, q] = pair.reshape(16, LANES).astype(BF16)
        main.start()

    out_wave(0)
    dx_first(True)
    dx_first(False)
    out_wave(1)
    for away in offsets:
        landed(rdw.at[away - 1], R_DW + away - 1)
    for i in range(3):
        total = (pdw[y, i] + rdw[0, i] + rdw[1, i] + rdw[2, i]) * norm
        for j in range(3):
            dw_v[i, j] = total[:, 128 * j : 128 * j + 128]
    stores = [
        pltpu.make_async_copy(dw_v, dw_o, fs.at[0]),
        pltpu.make_async_copy(dx_v, dx_o, fs.at[1]),
        pltpu.make_async_copy(out_v, out_o, fs.at[2]),
    ]
    stores[0].start()

    dx_finish()
    dx_v[...] = (pdx[z + 1] + rdx[0, 3] + rdx[1, 3]).astype(BF16)
    stores[1].start()

    inside = jnp.where(k == 0, x > 0, x < NX - 1)
    for w in range(WAVES):
        for copy in out_copies(w):
            copy.wait_recv()
        out_v[pl.ds(1 - k, 7), 16 * w : 16 * w + 16] = orx[w]
        row = (oe[w] + jnp.where(inside, oh[w], 0.0)).reshape(16, LANES)
        out_v[7 * k, 16 * w : 16 * w + 16] = row.astype(BF16)
    stores[2].start()

    @pl.when(off_diag)
    def _():
        main_copy(0).wait_send()

    left_by(ob, S_OM)
    left_by(oe, S_OE)
    left_by(xg.at[pl.ds(0, 7)], S_X)
    left_by(wg.at[pl.ds(0, 3)], S_W)
    left_by(xg.at[pl.ds(0, 3)], S_T)
    left_by(gin.at[pl.ds(0, 4)], S_H)
    left_by(gg.at[k], S_C)
    left_by(pdx.at[pl.ds(0, 7)], S_DX)
    left_by(pdw.at[pl.ds(0, 3)], S_DW)
    left_by(pk.at[pl.ds(0, 3)], S_O)
    left_by(pk, S_OC)
    left_by(oh, S_OH)
    for store in stores:
        store.wait()


def place(*refs):
    sems = refs[6]
    copies = [pltpu.make_async_copy(refs[i], refs[i + 3], sems.at[i]) for i in range(3)]
    for copy in copies:
        copy.start()
    for copy in copies:
        copy.wait()


def body(inputs, weights, cotangent):
    norm = 1.0 / math.sqrt(inputs.shape[0] * cotangent.shape[1] * 8 * inputs.shape[2])
    vmem = pl.BlockSpec(memory_space=pltpu.VMEM)
    hbm = pl.BlockSpec(memory_space=pl.ANY)
    out, dx, dw = pl.pallas_call(
        functools.partial(kernel, norm),
        out_shape=(
            pltpu.VMEM((8, 32, 128), BF16),
            pltpu.VMEM((2, 128, 128), BF16),
            pltpu.VMEM((3, 3, 32, 128), F32),
        ),
        in_specs=[hbm] * 3,
        out_specs=[hbm] * 3,
        scratch_shapes=[
            pltpu.VMEM((8, 32, 128), BF16),
            pltpu.VMEM((2, 128, 128), BF16),
            pltpu.VMEM((3, 3, 32, 128), F32),
            pltpu.VMEM((8, 32, 128), BF16),
            pltpu.VMEM((8, 2, 128, 128), BF16),
            pltpu.VMEM((4, 3, 3, 32, 128), BF16),
            pltpu.VMEM((2, 4, 9, 32, 128), BF16),
            pltpu.VMEM((2048, 384), BF16),
            pltpu.VMEM((2304, 384), BF16),
            pltpu.VMEM((128, 2304), BF16),
            pltpu.VMEM((384, 384), BF16),
            pltpu.VMEM((384, 384), BF16),
            pltpu.VMEM((10, 2, 128, 128), F32),
            pltpu.VMEM((2, 4, 2, 128, 128), F32),
            pltpu.VMEM((384, 384), F32),
            pltpu.VMEM((4, 3, 32, 384), F32),
            pltpu.VMEM((3, 3, 32, 384), F32),
            pltpu.VMEM((2, 4, PIECES, 9, 8, 128), F32),
            pltpu.VMEM((4, PIECES, 9, 8, 128), F32),
            pltpu.VMEM((3, PIECES, 9, 8, 128), F32),
            pltpu.VMEM((WAVES, 7, 16, 128), BF16),
            pltpu.VMEM((WAVES, 7, 16, 128), BF16),
            pltpu.VMEM((WAVES, 2, 8, 128), F32),
            pltpu.VMEM((WAVES, 2, 8, 128), F32),
            pltpu.SemaphoreType.DMA((N_SEND,)),
            pltpu.SemaphoreType.DMA((N_RECV,)),
            pltpu.SemaphoreType.DMA((3,)),
            pltpu.SemaphoreType.DMA((3,)),
        ],
        compiler_params=pltpu.CompilerParams(collective_id=0, has_side_effects=True),
        name="conv_layer",
    )(inputs[0], weights, cotangent[0])
    out, dx, dw = pl.pallas_call(
        place,
        out_shape=(
            jax.ShapeDtypeStruct((8, 32, 128), BF16),
            jax.ShapeDtypeStruct((2, 128, 128), BF16),
            jax.ShapeDtypeStruct((3, 3, 32, 128), F32),
        ),
        in_specs=[vmem] * 3,
        out_specs=[hbm] * 3,
        scratch_shapes=[pltpu.SemaphoreType.DMA((3,))],
        name="place_results",
    )(*(pltpu.with_memory_space_constraint(v, pltpu.VMEM) for v in (out, dx, dw)))
    return out[None], dx[None], dw


def solution(mesh):
    return jax.shard_map(
        body,
        mesh=mesh,
        in_specs=(
            P(None, "filt", None, "chan"),
            P(None, None, "filt", "chan"),
            P(None, "chan", "filt", None),
        ),
        out_specs=(
            P(None, "chan", "filt", None),
            P(None, "filt", None, "chan"),
            P(None, None, "filt", "chan"),
        ),
        check_vma=False,
    )
```

```python
import functools
import math

import jax
import jax.numpy as jnp
from jax import lax
from jax.experimental import pallas as pl
from jax.experimental.pallas import tpu as pltpu
from jax.sharding import PartitionSpec as P

MESH = pl.DeviceIdType.MESH
BF16 = jnp.bfloat16
F32 = jnp.float32

NX, NY, NZ = 4, 4, 8
LANES = 128

PIECES = 4
WAVES = 2


def layout(*sizes):
    return [sum(sizes[:i]) for i in range(len(sizes) + 1)]


R_X, R_W, R_T, R_C, R_DX, R_DW, R_O, R_OC, R_OM, R_OE, R_OH, N_RECV = layout(
    12, NY - 1, NY, NX, 2 * (3 * PIECES + PIECES // 2), NY - 1, (NX - 1) * WAVES,
    WAVES, WAVES, WAVES, WAVES,
)
S_X, S_W, S_T, S_SWAP, S_H, S_C, S_DX, S_DW, S_O, S_OC, S_OM, S_OE, S_OH, N_SEND = layout(*[1] * 13)


def kernel(
    norm,
    x_in, w_in, g_in,
    out_o, dx_o, dw_o,
    out_v, dx_v, dw_v, gin, xg, wg, gg, x3, y3, dyn, wf, wb,
    pdx, rdx, acc, pdw, rdw, po, rk, ro, ob, orx, oe, oh,
    ss, rs, ls, fs,
):
    chan = lax.axis_index("chan")
    filt = lax.axis_index("filt")
    x, k = lax.div(chan, 2), lax.rem(chan, 2)
    y, z = lax.div(filt, NZ), lax.rem(filt, NZ)

    def dev(dx, dk, dy, dz):
        return (dx * 2 + dk, dy * NZ + dz)

    def mod(v, n):
        return lax.rem(v + n, n)

    def along_x(i):
        return dev(mod(x + i, NX), k, y, z)

    def along_y(i):
        return dev(x, k, mod(y + i, NY), z)

    def along_z(i):
        return dev(x, k, y, mod(z + i, NZ))

    other = dev(x, 1 - k, y, z)
    off_diag = x != y
    step = 2 * k - 1

    def owner(i, row):
        inner = lax.div(row * (NY - 1 - row), 2)
        return lax.rem(inner * (2 * row + 2 - i) + (1 - inner) * (i + 2) + 2 * NX, NX)

    mine = owner(x, y)
    out_to = dev(y, k, mine, z)
    out_from = dev(owner(y, x), k, x, z)
    above, across = mod(y + step, NX), mod(x + step, NY)
    out_halo_to = dev(above, 1 - k, mine, z)
    out_halo_from = dev(owner(y, across), 1 - k, across, z)

    loads = [
        pltpu.make_async_copy(g_in, gin, ls.at[0]),
        pltpu.make_async_copy(x_in, xg.at[z], ls.at[1]),
        pltpu.make_async_copy(w_in, wg.at[y], ls.at[2]),
    ]
    for load in loads:
        load.start()

    barrier = pltpu.get_barrier_semaphore()

    def greet(peer):
        pl.semaphore_signal(barrier, inc=1, device_id=peer, device_id_type=MESH)

    for i in (2, 1, 3, 0):
        b = mod(y + i, NY)
        greet(dev(mod(y + step, NX), 1 - k, b, z))
        if i:
            greet(dev(y, k, mod(x + i, NY), z))
    for peer in (
        *[along_x(i) for i in (1, 2, 3)], *[along_y(i) for i in (1, 2, 3)],
        *[along_z(i) for i in (-2, -1, 1, 2)], other, out_from, out_halo_from,
    ):
        greet(peer)

    @pl.when(off_diag)
    def _():
        greet(dev(y, k, x, z))

    pl.semaphore_wait(barrier, jnp.where(off_diag, 21, 20))
    for load in loads:
        load.wait()

    def rcopy(src, dst, send, recv, target):
        return pltpu.make_async_remote_copy(
            src_ref=src, dst_ref=dst, send_sem=ss.at[send], recv_sem=rs.at[recv],
            device_id=target, device_id_type=MESH,
        )

    def push(src, dst, send, recv, target):
        rcopy(src, dst, send, recv, target).start()

    def landed(dst, recv):
        rcopy(dst, dst, S_X, recv, other).wait_recv()

    def left_by(size, send):
        rcopy(size, size, send, R_X, other).wait_send()

    ways = (1, -1)

    def x_send(d, away, reach, row, slot):
        ref = xg.at[mod(z - ways[d] * away, NZ), row]
        push(ref, ref, S_X, R_X + 6 * d + slot, along_z(ways[d] * reach))

    def x_landed(d, away, row, slot):
        landed(xg.at[mod(z - ways[d] * away, NZ), row], R_X + 6 * d + slot)

    def x_start():
        for turn in range(2):
            for d in range(2):
                x_send(d, 0, 2, d if turn == 0 else 1 - d, turn)
        for d in range(2):
            block = xg.at[z]
            push(block, block, S_X, R_X + 6 * d + 2, along_z(ways[d]))

    def x_relay():
        for turn in range(2):
            for d in range(2):
                row = d if turn == 0 else 1 - d
                x_landed(d, 2, row, turn)
                if turn == 0:
                    x_send(d, 2, 2, row, 3)
                x_send(d, 2, 1, row, 4 + turn)

    def x_near():
        for d in range(2):
            landed(xg.at[mod(z - ways[d], NZ)], R_X + 6 * d + 2)

    def x_third():
        for turn in range(2):
            for d in range(2):
                x_landed(d, 3, d if turn == 0 else 1 - d, 4 + turn)

    def x_fourth():
        for d in range(2):
            x_landed(d, 4, d, 3)

    half = PIECES // 2
    far_pieces = (range(half), range(half, PIECES))

    def dx_cut(ref, piece):
        return ref.at[piece // 2, pl.ds(64 * (piece % 2), 64)]

    def dx_sem(d, stage, piece):
        return R_DX + d * (3 * PIECES + half) + (piece - d * half if stage == 0 else half + (stage - 1) * PIECES + piece)

    def dx_send(d, away, reach, stage, piece):
        push(
            dx_cut(pdx.at[mod(z + ways[d] * away, NZ) + 1], piece),
            dx_cut(rdx.at[d, stage], piece), S_DX, dx_sem(d, stage, piece),
            along_z(ways[d] * reach),
        )

    def dx_order(d):
        return (*far_pieces[d], *far_pieces[1 - d])

    def dx_fourth():
        for i in range(half):
            for d in range(2):
                dx_send(d, 4, 2, 0, far_pieces[d][i])

    def dx_third():
        for i in range(PIECES):
            for d in range(2):
                dx_send(d, 3, 1, 1, dx_order(d)[i])

    def dx_add(d, away, stage, piece):
        term = dx_cut(rdx.at[d, stage], piece)
        landed(term, dx_sem(d, stage, piece))
        dx_cut(pdx.at[mod(z + ways[d] * away, NZ) + 1], piece)[...] += term[...]

    def dx_second(far):
        for i in range(half):
            for d in range(2):
                piece = far_pieces[d if far else 1 - d][i]
                dx_add(d, 2, 1, piece)
                if far:
                    dx_add(d, 2, 0, piece)
                dx_send(d, 2, 1, 2, piece)

    def dx_first(far):
        for i in range(half):
            for d in range(2):
                piece = far_pieces[d if far else 1 - d][i]
                dx_add(d, 1, 2, piece)
                dx_send(d, 1, 1, 3, piece)

    def dx_finish():
        for d in range(2):
            for piece in range(PIECES):
                landed(dx_cut(rdx.at[d, 3], piece), dx_sem(d, 3, piece))

    pk = po.at[k]
    per_wave = PIECES // WAVES
    offsets = (2, 1, 3)

    def o_part(w, i):
        return pk.at[owner(mod(x + i, NX), y), pl.ds(w * per_wave, per_wave)]

    def o_slot(w, i):
        return ro.at[i - 1, pl.ds(w * per_wave, per_wave)], R_O + w * (NX - 1) + i - 1

    def o_send(w, i):
        dst, recv = o_slot(w, i)
        push(o_part(w, i), dst, S_O, recv, along_x(i))

    def main_copy(i):
        return rcopy(
            gin, gg.at[k, y, pl.ds(1 - k, 8)], S_T if i else S_SWAP, R_T + y,
            dev(mod(x + i, NX), k, x, z),
        )

    def self_copy():
        return pltpu.make_async_copy(gin, gg.at[k, y, pl.ds(1 - k, 8)], ls.at[0])

    for i in (2, 1, 3):
        main_copy(i).start()

    @pl.when(off_diag)
    def _():
        main_copy(0).start()

    @pl.when(jnp.logical_not(off_diag))
    def _():
        self_copy().start()

    for i in range(NX):
        push(
            gin.at[7 * k], gg.at[1 - k, y, 8 * (1 - k)], S_H, R_T + y,
            dev(mod(x + i, NX), 1 - k, mod(x + step, NY), z),
        )
    for i in offsets:
        push(wg.at[y], wg.at[y], S_W, R_W + i - 1, along_y(i))

    def cot_block(i):
        b = mod(x + i, NY)
        if i:
            landed(gg.at[k, b], R_T + b)
        else:

            @pl.when(off_diag)
            def _():
                landed(gg.at[k, b], R_T + b)

            @pl.when(jnp.logical_not(off_diag))
            def _():
                landed(gg.at[k, b, 8 * k], R_T + b)
                self_copy().wait()

        push(gg.at[k, b], gg.at[k, b], S_C, R_C + i, other)

    col = lax.broadcasted_iota(jnp.int32, (LANES, LANES), 0)

    def shifts(v):
        before = jnp.where(col == 0, 0.0, pltpu.roll(v, 1, 0))
        after = jnp.where(col == LANES - 1, 0.0, pltpu.roll(v, LANES - 1, 0))
        return before.astype(BF16), after.astype(BF16)

    def y_rows(half):
        def row(ql):
            q = half * 9 + ql
            outside = jnp.logical_or(
                jnp.logical_and(q == 0, y == 0), jnp.logical_and(q == 17, y == NY - 1)
            )
            v = gg[half, :, ql].reshape(LANES, LANES).astype(F32)
            v = jnp.where(outside, 0.0, v)
            at = pl.multiple_of(q * LANES, LANES)
            dyn[:, pl.ds(at, LANES)] = v.astype(BF16)
            t = v.T
            before, after = shifts(t)
            y3[pl.ds(at, LANES), 0:128] = after
            y3[pl.ds(at, LANES), 128:256] = t.astype(BF16)
            y3[pl.ds(at, LANES), 256:384] = before

        for ql in range(9):
            row(ql)

    def x_block(i):
        block = mod(z + i, NZ)
        for u in range(2):
            v16 = xg[block, u]
            before, after = shifts(v16.astype(F32))
            at = pl.multiple_of((block * 2 + u) * LANES, LANES)
            x3[pl.ds(at, LANES), 0:128] = before
            x3[pl.ds(at, LANES), 128:256] = v16
            x3[pl.ds(at, LANES), 256:384] = after

    far = mod(z + NZ // 2, NZ)

    def dx_pair(i):
        t = mod(far + i, 9)
        at = pl.multiple_of(t * 2 * LANES, 2 * LANES)
        r = jnp.dot(y3[pl.ds(at, 2 * LANES), :], wb[...], preferred_element_type=F32)
        r0, r1 = r[:LANES], r[LANES:]
        pdx[t, 0] += r0[:, 0:128]
        pdx[t, 1] += r0[:, 128:256] + r1[:, 0:128]
        pdx[t + 1, 0] += r0[:, 256:384] + r1[:, 128:256]
        pdx[t + 1, 1] += r1[:, 256:384]

    tile = (NX, PIECES // WAVES, 8, LANES)

    def out_pair(i, w):
        t = (1 - k) * 7 + step * i
        at = pl.multiple_of(t * 2 * LANES, 2 * LANES)
        r = lax.dot_general(
            wf[192 * w : 192 * w + 192], x3[pl.ds(at, 2 * LANES), :], (((1,), (1,)), ((), ())),
            preferred_element_type=F32,
        )
        r0, r1 = r[:, :LANES], r[:, LANES:]

        def row(q):
            return po.at[lax.div(q, 9), :, pl.ds(w * per_wave, per_wave), lax.rem(q, 9)]

        row(2 * t)[...] += r0[128:192].reshape(tile)
        row(2 * t + 1)[...] += (r0[64:128] + r1[128:192]).reshape(tile)
        row(2 * t + 2)[...] += (r0[0:64] + r1[64:128]).reshape(tile)
        row(2 * t + 3)[...] += r1[0:64].reshape(tile)

    def dw_all():
        lhs = jnp.concatenate(
            [dyn[:, (2 - i) * LANES : (18 - i) * LANES] for i in range(3)], axis=0
        )
        acc[...] = jnp.dot(lhs, x3[...], preferred_element_type=F32)
        for b in range(NY):
            for i in range(3):
                pdw[b, i] = acc[128 * i + 32 * b : 128 * i + 32 * b + 32, :]
        for away in offsets:
            push(
                pdw.at[mod(y + away, NY)], rdw.at[away - 1], S_DW, R_DW + away - 1, along_y(away)
            )

    x_start()
    pdx[...] = jnp.zeros_like(pdx)
    po[...] = jnp.zeros_like(po)
    x_block(0)
    x_relay()
    for i in (0, 1, 3, 2):
        cot_block(i)
    x_near()
    for i in (1, -1, 2, -2):
        x_block(i)
    y_rows(k)
    for i in (0, 1, 3, 2):
        landed(gg.at[1 - k, mod(x + i, NY)], R_C + i)
    y_rows(1 - k)
    for i in offsets:
        landed(wg.at[mod(y - i, NY)], R_W + i - 1)
    for b in range(NY):
        for i in range(3):
            for j in range(3):
                tap = wg[b, i, j]
                for w in range(WAVES):
                    at = w * 192 + i * 64 + b * 16
                    wf[at : at + 16, j * 128 : j * 128 + 128] = tap[16 * w : 16 * w + 16]
                wb[j * 128 + b * 32 : j * 128 + b * 32 + 32, i * 128 : i * 128 + 128] = tap

    for i in (0, 1):
        dx_pair(i)
    dx_fourth()
    for i in (2, 3, 7, 8):
        dx_pair(i)
    dx_third()
    x_third()
    for i in (3, -3):
        x_block(i)
    x_fourth()
    x_block(4)
    for w in range(WAVES):
        for i in range(5):
            out_pair(i, w)
        part = pl.ds(w * per_wave, per_wave)
        push(po.at[1 - k, :, part], rk.at[:, part], S_OC, R_OC + w, other)
    for w in range(WAVES):
        for i in range(5, 8):
            out_pair(i, w)
    def core_sum(w):
        part = pl.ds(w * per_wave, per_wave)
        landed(rk.at[:, part], R_OC + w)
        for i in (*offsets, 0):
            b = owner(mod(x + i, NX), y)
            pk.at[b, part][...] += rk[b, w * per_wave : (w + 1) * per_wave]
            if i:
                o_send(w, i)

    core_sum(0)
    for i in (4, 5, 6):
        dx_pair(i)
    core_sum(1)
    dw_all()
    dx_second(True)
    dx_second(False)

    sums = po.at[k, mine]

    def out_copies(w):
        part = pl.ds(w * per_wave, per_wave)
        return (
            rcopy(ob.at[w], orx.at[w], S_OM, R_OM + w, out_to),
            rcopy(sums.at[part, 7 * k + 1 - k], oe.at[w], S_OE, R_OE + w, out_to),
            rcopy(sums.at[part, 8 * k], oh.at[w], S_OH, R_OH + w, out_halo_to),
        )

    def out_wave(w):
        for i in offsets:
            landed(*o_slot(w, i))
        for h in range(w * per_wave, (w + 1) * per_wave):
            for q in range(9):
                sums[h, q] += ro[0, h, q] + ro[1, h, q] + ro[2, h, q]
        main, edge, halo = out_copies(w)
        halo.start()
        edge.start()
        for q in range(7):
            pair = sums[w * per_wave : (w + 1) * per_wave, q + 2 * (1 - k)]
            ob[w, q] = pair.reshape(16, LANES).astype(BF16)
        main.start()

    out_wave(0)
    dx_first(True)
    dx_first(False)
    out_wave(1)
    for away in offsets:
        landed(rdw.at[away - 1], R_DW + away - 1)
    for i in range(3):
        total = (pdw[y, i] + rdw[0, i] + rdw[1, i] + rdw[2, i]) * norm
        for j in range(3):
            dw_v[i, j] = total[:, 128 * j : 128 * j + 128]
    stores = [
        pltpu.make_async_copy(dw_v, dw_o, fs.at[0]),
        pltpu.make_async_copy(dx_v, dx_o, fs.at[1]),
        pltpu.make_async_copy(out_v, out_o, fs.at[2]),
    ]
    stores[0].start()

    dx_finish()
    dx_v[...] = (pdx[z + 1] + rdx[0, 3] + rdx[1, 3]).astype(BF16)
    stores[1].start()

    inside = jnp.where(k == 0, x > 0, x < NX - 1)
    for w in range(WAVES):
        for copy in out_copies(w):
            copy.wait_recv()
        out_v[pl.ds(1 - k, 7), 16 * w : 16 * w + 16] = orx[w]
        row = (oe[w] + jnp.where(inside, oh[w], 0.0)).reshape(16, LANES)
        out_v[7 * k, 16 * w : 16 * w + 16] = row.astype(BF16)
    stores[2].start()

    @pl.when(off_diag)
    def _():
        main_copy(0).wait_send()

    left_by(ob, S_OM)
    left_by(oe, S_OE)
    left_by(xg.at[pl.ds(0, 7)], S_X)
    left_by(wg.at[pl.ds(0, 3)], S_W)
    left_by(xg.at[pl.ds(0, 3)], S_T)
    left_by(gin.at[pl.ds(0, 4)], S_H)
    left_by(gg.at[k], S_C)
    left_by(pdx.at[pl.ds(0, 7)], S_DX)
    left_by(pdw.at[pl.ds(0, 3)], S_DW)
    left_by(pk.at[pl.ds(0, 3)], S_O)
    left_by(pk, S_OC)
    left_by(oh, S_OH)
    for store in stores:
        store.wait()


def place(*refs):
    sems = refs[6]
    copies = [pltpu.make_async_copy(refs[i], refs[i + 3], sems.at[i]) for i in range(3)]
    for copy in copies:
        copy.start()
    for copy in copies:
        copy.wait()


def body(inputs, weights, cotangent):
    norm = 1.0 / math.sqrt(inputs.shape[0] * cotangent.shape[1] * 8 * inputs.shape[2])
    vmem = pl.BlockSpec(memory_space=pltpu.VMEM)
    hbm = pl.BlockSpec(memory_space=pl.ANY)
    out, dx, dw = pl.pallas_call(
        functools.partial(kernel, norm),
        out_shape=(
            pltpu.VMEM((8, 32, 128), BF16),
            pltpu.VMEM((2, 128, 128), BF16),
            pltpu.VMEM((3, 3, 32, 128), F32),
        ),
        in_specs=[hbm] * 3,
        out_specs=[hbm] * 3,
        scratch_shapes=[
            pltpu.VMEM((8, 32, 128), BF16),
            pltpu.VMEM((2, 128, 128), BF16),
            pltpu.VMEM((3, 3, 32, 128), F32),
            pltpu.VMEM((8, 32, 128), BF16),
            pltpu.VMEM((8, 2, 128, 128), BF16),
            pltpu.VMEM((4, 3, 3, 32, 128), BF16),
            pltpu.VMEM((2, 4, 9, 32, 128), BF16),
            pltpu.VMEM((2048, 384), BF16),
            pltpu.VMEM((2304, 384), BF16),
            pltpu.VMEM((128, 2304), BF16),
            pltpu.VMEM((384, 384), BF16),
            pltpu.VMEM((384, 384), BF16),
            pltpu.VMEM((10, 2, 128, 128), F32),
            pltpu.VMEM((2, 4, 2, 128, 128), F32),
            pltpu.VMEM((384, 384), F32),
            pltpu.VMEM((4, 3, 32, 384), F32),
            pltpu.VMEM((3, 3, 32, 384), F32),
            pltpu.VMEM((2, 4, PIECES, 9, 8, 128), F32),
            pltpu.VMEM((4, PIECES, 9, 8, 128), F32),
            pltpu.VMEM((3, PIECES, 9, 8, 128), F32),
            pltpu.VMEM((WAVES, 7, 16, 128), BF16),
            pltpu.VMEM((WAVES, 7, 16, 128), BF16),
            pltpu.VMEM((WAVES, 2, 8, 128), F32),
            pltpu.VMEM((WAVES, 2, 8, 128), F32),
            pltpu.SemaphoreType.DMA((N_SEND,)),
            pltpu.SemaphoreType.DMA((N_RECV,)),
            pltpu.SemaphoreType.DMA((3,)),
            pltpu.SemaphoreType.DMA((3,)),
        ],
        compiler_params=pltpu.CompilerParams(collective_id=0, has_side_effects=True),
        name="conv_layer",
    )(inputs[0], weights, cotangent[0])
    out, dx, dw = pl.pallas_call(
        place,
        out_shape=(
            jax.ShapeDtypeStruct((8, 32, 128), BF16),
            jax.ShapeDtypeStruct((2, 128, 128), BF16),
            jax.ShapeDtypeStruct((3, 3, 32, 128), F32),
        ),
        in_specs=[vmem] * 3,
        out_specs=[hbm] * 3,
        scratch_shapes=[pltpu.SemaphoreType.DMA((3,))],
        name="place_results",
    )(*(pltpu.with_memory_space_constraint(v, pltpu.VMEM) for v in (out, dx, dw)))
    return out[None], dx[None], dw


def solution(mesh):
    return jax.shard_map(
        body,
        mesh=mesh,
        in_specs=(
            P(None, "filt", None, "chan"),
            P(None, None, "filt", "chan"),
            P(None, "chan", "filt", None),
        ),
        out_specs=(
            P(None, "chan", "filt", None),
            P(None, "filt", None, "chan"),
            P(None, None, "filt", "chan"),
        ),
        check_vma=False,
    )
```

```python
import functools
import math

import jax
import jax.numpy as jnp
from jax import lax
from jax.experimental import pallas as pl
from jax.experimental.pallas import tpu as pltpu
from jax.sharding import PartitionSpec as P

MESH = pl.DeviceIdType.MESH
BF16 = jnp.bfloat16
F32 = jnp.float32

NX, NY, NZ = 4, 4, 8
LANES = 128

PIECES = 4
WAVES = 2


def layout(*sizes):
    return [sum(sizes[:i]) for i in range(len(sizes) + 1)]


R_X, R_W, R_T, R_C, R_DX, R_DW, R_O, R_OC, R_OM, R_OE, R_OH, N_RECV = layout(
    12, NY - 1, NY, NX, 2 * (3 * PIECES + PIECES // 2), NY - 1, (NX - 1) * WAVES,
    WAVES, WAVES, WAVES, WAVES,
)
S_SWAP, S_X, S_C, S_DX, N_SEND = range(5)
S_W = S_OM = S_X
S_DW = S_O = S_OC = S_C
S_T = S_H = S_OE = S_OH = S_DX


def kernel(
    norm,
    x_in, w_in, g_in,
    out_o, dx_o, dw_o,
    out_v, dx_v, dw_v, gin, xg, wg, gg, x3, y3, dyn, wf, wb,
    pdx, rdx, acc, pdw, rdw, po, rk, ro, ob, orx, oe, oh,
    ss, rs, ls, fs,
):
    chan = lax.axis_index("chan")
    filt = lax.axis_index("filt")
    x, k = lax.div(chan, 2), lax.rem(chan, 2)
    y, z = lax.div(filt, NZ), lax.rem(filt, NZ)

    def dev(dx, dk, dy, dz):
        return (dx * 2 + dk, dy * NZ + dz)

    def mod(v, n):
        return lax.rem(v + n, n)

    def along_x(i):
        return dev(mod(x + i, NX), k, y, z)

    def along_y(i):
        return dev(x, k, mod(y + i, NY), z)

    def along_z(i):
        return dev(x, k, y, mod(z + i, NZ))

    other = dev(x, 1 - k, y, z)
    off_diag = x != y
    step = 2 * k - 1

    def owner(i, row):
        inner = lax.div(row * (NY - 1 - row), 2)
        return lax.rem(inner * (2 * row + 2 - i) + (1 - inner) * (i + 2) + 2 * NX, NX)

    mine = owner(x, y)
    out_to = dev(y, k, mine, z)
    out_from = dev(owner(y, x), k, x, z)
    above, across = mod(y + step, NX), mod(x + step, NY)
    out_halo_to = dev(above, 1 - k, mine, z)
    out_halo_from = dev(owner(y, across), 1 - k, across, z)

    loads = [
        pltpu.make_async_copy(g_in, gin, ls.at[0]),
        pltpu.make_async_copy(x_in, xg.at[z], ls.at[1]),
        pltpu.make_async_copy(w_in, wg.at[y], ls.at[2]),
    ]
    for load in loads:
        load.start()

    barrier = pltpu.get_barrier_semaphore()

    def greet(peer):
        pl.semaphore_signal(barrier, inc=1, device_id=peer, device_id_type=MESH)

    for i in (2, 1, 3, 0):
        b = mod(y + i, NY)
        greet(dev(mod(y + step, NX), 1 - k, b, z))
        if i:
            greet(dev(y, k, mod(x + i, NY), z))
    for peer in (
        *[along_x(i) for i in (1, 2, 3)], *[along_y(i) for i in (1, 2, 3)],
        *[along_z(i) for i in (-2, -1, 1, 2)], other, out_from, out_halo_from,
    ):
        greet(peer)

    @pl.when(off_diag)
    def _():
        greet(dev(y, k, x, z))

    pl.semaphore_wait(barrier, jnp.where(off_diag, 21, 20))
    for load in loads:
        load.wait()

    def rcopy(src, dst, send, recv, target):
        return pltpu.make_async_remote_copy(
            src_ref=src, dst_ref=dst, send_sem=ss.at[send], recv_sem=rs.at[recv],
            device_id=target, device_id_type=MESH,
        )

    def push(src, dst, send, recv, target):
        rcopy(src, dst, send, recv, target).start()

    def landed(dst, recv):
        rcopy(dst, dst, S_X, recv, other).wait_recv()

    def left_by(size, send):
        rcopy(size, size, send, R_X, other).wait_send()

    ways = (1, -1)

    def x_send(d, away, reach, row, slot):
        ref = xg.at[mod(z - ways[d] * away, NZ), row]
        push(ref, ref, S_X, R_X + 6 * d + slot, along_z(ways[d] * reach))

    def x_landed(d, away, row, slot):
        landed(xg.at[mod(z - ways[d] * away, NZ), row], R_X + 6 * d + slot)

    def x_start():
        for turn in range(2):
            for d in range(2):
                x_send(d, 0, 2, d if turn == 0 else 1 - d, turn)
        for d in range(2):
            block = xg.at[z]
            push(block, block, S_X, R_X + 6 * d + 2, along_z(ways[d]))

    def x_relay():
        for turn in range(2):
            for d in range(2):
                row = d if turn == 0 else 1 - d
                x_landed(d, 2, row, turn)
                if turn == 0:
                    x_send(d, 2, 2, row, 3)
                x_send(d, 2, 1, row, 4 + turn)

    def x_near():
        for d in range(2):
            landed(xg.at[mod(z - ways[d], NZ)], R_X + 6 * d + 2)

    def x_third():
        for turn in range(2):
            for d in range(2):
                x_landed(d, 3, d if turn == 0 else 1 - d, 4 + turn)

    def x_fourth():
        for d in range(2):
            x_landed(d, 4, d, 3)

    half = PIECES // 2
    far_pieces = (range(half), range(half, PIECES))

    def dx_cut(ref, piece):
        return ref.at[piece // 2, pl.ds(64 * (piece % 2), 64)]

    def dx_sem(d, stage, piece):
        return R_DX + d * (3 * PIECES + half) + (piece - d * half if stage == 0 else half + (stage - 1) * PIECES + piece)

    def dx_send(d, away, reach, stage, piece):
        push(
            dx_cut(pdx.at[mod(z + ways[d] * away, NZ) + 1], piece),
            dx_cut(rdx.at[d, stage], piece), S_DX, dx_sem(d, stage, piece),
            along_z(ways[d] * reach),
        )

    def dx_order(d):
        return (*far_pieces[1 - d], *far_pieces[d])

    def dx_fourth():
        for i in range(half):
            for d in range(2):
                dx_send(d, 4, 2, 0, far_pieces[d][i])

    def dx_third():
        for i in range(PIECES):
            for d in range(2):
                dx_send(d, 3, 1, 1, dx_order(d)[i])

    def dx_add(d, away, stage, piece):
        term = dx_cut(rdx.at[d, stage], piece)
        landed(term, dx_sem(d, stage, piece))
        dx_cut(pdx.at[mod(z + ways[d] * away, NZ) + 1], piece)[...] += term[...]

    def dx_second(far):
        for i in range(half):
            for d in range(2):
                piece = far_pieces[d if far else 1 - d][i]
                dx_add(d, 2, 1, piece)
                if far:
                    dx_add(d, 2, 0, piece)
                dx_send(d, 2, 1, 2, piece)

    def dx_first(far):
        for i in range(half):
            for d in range(2):
                piece = far_pieces[d if far else 1 - d][i]
                dx_add(d, 1, 2, piece)
                dx_send(d, 1, 1, 3, piece)

    def dx_finish():
        for d in range(2):
            for piece in range(PIECES):
                landed(dx_cut(rdx.at[d, 3], piece), dx_sem(d, 3, piece))

    pk = po.at[k]
    per_wave = PIECES // WAVES
    offsets = (2, 1, 3)

    def o_part(w, i):
        return pk.at[owner(mod(x + i, NX), y), pl.ds(w * per_wave, per_wave)]

    def o_slot(w, i):
        return ro.at[i - 1, pl.ds(w * per_wave, per_wave)], R_O + w * (NX - 1) + i - 1

    def o_send(w, i):
        dst, recv = o_slot(w, i)
        push(o_part(w, i), dst, S_O, recv, along_x(i))

    def main_copy(i):
        return rcopy(
            gin, gg.at[k, y, pl.ds(1 - k, 8)], S_T if i else S_SWAP, R_T + y,
            dev(mod(x + i, NX), k, x, z),
        )

    def self_copy():
        return pltpu.make_async_copy(gin, gg.at[k, y, pl.ds(1 - k, 8)], ls.at[0])

    for i in (2, 1, 3):
        main_copy(i).start()

    @pl.when(off_diag)
    def _():
        main_copy(0).start()

    @pl.when(jnp.logical_not(off_diag))
    def _():
        self_copy().start()

    for i in range(NX):
        push(
            gin.at[7 * k], gg.at[1 - k, y, 8 * (1 - k)], S_H, R_T + y,
            dev(mod(x + i, NX), 1 - k, mod(x + step, NY), z),
        )
    for i in offsets:
        push(wg.at[y], wg.at[y], S_W, R_W + i - 1, along_y(i))

    def cot_block(i):
        b = mod(x + i, NY)
        if i:
            landed(gg.at[k, b], R_T + b)
        else:

            @pl.when(off_diag)
            def _():
                landed(gg.at[k, b], R_T + b)

            @pl.when(jnp.logical_not(off_diag))
            def _():
                landed(gg.at[k, b, 8 * k], R_T + b)
                self_copy().wait()

        push(gg.at[k, b], gg.at[k, b], S_C, R_C + i, other)

    col = lax.broadcasted_iota(jnp.int32, (LANES, LANES), 0)

    def shifts(v):
        before = jnp.where(col == 0, 0.0, pltpu.roll(v, 1, 0))
        after = jnp.where(col == LANES - 1, 0.0, pltpu.roll(v, LANES - 1, 0))
        return before.astype(BF16), after.astype(BF16)

    def y_rows(half):
        def row(ql):
            q = half * 9 + ql
            outside = jnp.logical_or(
                jnp.logical_and(q == 0, y == 0), jnp.logical_and(q == 17, y == NY - 1)
            )
            v = gg[half, :, ql].reshape(LANES, LANES).astype(F32)
            v = jnp.where(outside, 0.0, v)
            at = pl.multiple_of(q * LANES, LANES)
            dyn[:, pl.ds(at, LANES)] = v.astype(BF16)
            t = v.T
            before, after = shifts(t)
            y3[pl.ds(at, LANES), 0:128] = after
            y3[pl.ds(at, LANES), 128:256] = t.astype(BF16)
            y3[pl.ds(at, LANES), 256:384] = before

        for ql in range(9):
            row(ql)

    def x_block(i):
        block = mod(z + i, NZ)
        for u in range(2):
            v16 = xg[block, u]
            before, after = shifts(v16.astype(F32))
            at = pl.multiple_of((block * 2 + u) * LANES, LANES)
            x3[pl.ds(at, LANES), 0:128] = before
            x3[pl.ds(at, LANES), 128:256] = v16
            x3[pl.ds(at, LANES), 256:384] = after

    far = mod(z + NZ // 2, NZ)

    def dx_pair(i):
        t = mod(far + i, 9)
        at = pl.multiple_of(t * 2 * LANES, 2 * LANES)
        r = jnp.dot(y3[pl.ds(at, 2 * LANES), :], wb[...], preferred_element_type=F32)
        r0, r1 = r[:LANES], r[LANES:]
        pdx[t, 0] += r0[:, 0:128]
        pdx[t, 1] += r0[:, 128:256] + r1[:, 0:128]
        pdx[t + 1, 0] += r0[:, 256:384] + r1[:, 128:256]
        pdx[t + 1, 1] += r1[:, 256:384]

    tile = (NX, PIECES // WAVES, 8, LANES)

    def out_pair(i, w):
        t = (1 - k) * 7 + step * i
        at = pl.multiple_of(t * 2 * LANES, 2 * LANES)
        r = lax.dot_general(
            wf[192 * w : 192 * w + 192], x3[pl.ds(at, 2 * LANES), :], (((1,), (1,)), ((), ())),
            preferred_element_type=F32,
        )
        r0, r1 = r[:, :LANES], r[:, LANES:]

        def row(q):
            return po.at[lax.div(q, 9), :, pl.ds(w * per_wave, per_wave), lax.rem(q, 9)]

        row(2 * t)[...] += r0[128:192].reshape(tile)
        row(2 * t + 1)[...] += (r0[64:128] + r1[128:192]).reshape(tile)
        row(2 * t + 2)[...] += (r0[0:64] + r1[64:128]).reshape(tile)
        row(2 * t + 3)[...] += r1[0:64].reshape(tile)

    def dw_all():
        lhs = jnp.concatenate(
            [dyn[:, (2 - i) * LANES : (18 - i) * LANES] for i in range(3)], axis=0
        )
        acc[...] = jnp.dot(lhs, x3[...], preferred_element_type=F32)
        for b in range(NY):
            for i in range(3):
                pdw[b, i] = acc[128 * i + 32 * b : 128 * i + 32 * b + 32, :]
        for away in offsets:
            push(
                pdw.at[mod(y + away, NY)], rdw.at[away - 1], S_DW, R_DW + away - 1, along_y(away)
            )

    x_start()
    pdx[...] = jnp.zeros_like(pdx)
    po[...] = jnp.zeros_like(po)
    x_block(0)
    x_relay()
    for i in (0, 1, 3, 2):
        cot_block(i)
    x_near()
    for i in (1, -1, 2, -2):
        x_block(i)
    y_rows(k)
    for i in (0, 1, 3, 2):
        landed(gg.at[1 - k, mod(x + i, NY)], R_C + i)
    y_rows(1 - k)
    for i in offsets:
        landed(wg.at[mod(y - i, NY)], R_W + i - 1)
    for b in range(NY):
        for i in range(3):
            for j in range(3):
                tap = wg[b, i, j]
                for w in range(WAVES):
                    at = w * 192 + i * 64 + b * 16
                    wf[at : at + 16, j * 128 : j * 128 + 128] = tap[16 * w : 16 * w + 16]
                wb[j * 128 + b * 32 : j * 128 + b * 32 + 32, i * 128 : i * 128 + 128] = tap

    for i in (0, 1):
        dx_pair(i)
    dx_fourth()
    for i in (2, 3, 7, 8):
        dx_pair(i)
    dx_third()
    x_third()
    for i in (3, -3):
        x_block(i)
    x_fourth()
    x_block(4)
    for w in range(WAVES):
        for i in range(5):
            out_pair(i, w)
        part = pl.ds(w * per_wave, per_wave)
        push(po.at[1 - k, :, part], rk.at[:, part], S_OC, R_OC + w, other)
    for w in range(WAVES):
        for i in range(5, 8):
            out_pair(i, w)
    def core_sum(w):
        part = pl.ds(w * per_wave, per_wave)
        landed(rk.at[:, part], R_OC + w)
        for i in (*offsets, 0):
            b = owner(mod(x + i, NX), y)
            pk.at[b, part][...] += rk[b, w * per_wave : (w + 1) * per_wave]
            if i:
                o_send(w, i)

    core_sum(0)
    for i in (4, 5, 6):
        dx_pair(i)
    core_sum(1)
    dw_all()
    dx_second(False)
    dx_second(True)

    sums = po.at[k, mine]

    def out_copies(w):
        part = pl.ds(w * per_wave, per_wave)
        return (
            rcopy(ob.at[w], orx.at[w], S_OM, R_OM + w, out_to),
            rcopy(sums.at[part, 7 * k + 1 - k], oe.at[w], S_OE, R_OE + w, out_to),
            rcopy(sums.at[part, 8 * k], oh.at[w], S_OH, R_OH + w, out_halo_to),
        )

    def out_wave(w):
        for i in offsets:
            landed(*o_slot(w, i))
        for h in range(w * per_wave, (w + 1) * per_wave):
            for q in range(9):
                sums[h, q] += ro[0, h, q] + ro[1, h, q] + ro[2, h, q]
        main, edge, halo = out_copies(w)
        halo.start()
        edge.start()
        for q in range(7):
            pair = sums[w * per_wave : (w + 1) * per_wave, q + 2 * (1 - k)]
            ob[w, q] = pair.reshape(16, LANES).astype(BF16)
        main.start()

    out_wave(0)
    dx_first(False)
    dx_first(True)
    out_wave(1)
    for away in offsets:
        landed(rdw.at[away - 1], R_DW + away - 1)
    for i in range(3):
        total = (pdw[y, i] + rdw[0, i] + rdw[1, i] + rdw[2, i]) * norm
        for j in range(3):
            dw_v[i, j] = total[:, 128 * j : 128 * j + 128]
    stores = [
        pltpu.make_async_copy(dw_v, dw_o, fs.at[0]),
        pltpu.make_async_copy(dx_v, dx_o, fs.at[1]),
        pltpu.make_async_copy(out_v, out_o, fs.at[2]),
    ]
    stores[0].start()

    dx_finish()
    dx_v[...] = (pdx[z + 1] + rdx[0, 3] + rdx[1, 3]).astype(BF16)
    stores[1].start()

    inside = jnp.where(k == 0, x > 0, x < NX - 1)
    for w in range(WAVES):
        for copy in out_copies(w):
            copy.wait_recv()
        out_v[pl.ds(1 - k, 7), 16 * w : 16 * w + 16] = orx[w]
        row = (oe[w] + jnp.where(inside, oh[w], 0.0)).reshape(16, LANES)
        out_v[7 * k, 16 * w : 16 * w + 16] = row.astype(BF16)
    stores[2].start()

    @pl.when(off_diag)
    def _():
        main_copy(0).wait_send()

    left_by(y3.at[pl.ds(0, 960)], S_X)
    left_by(y3, S_C)
    left_by(pdx.at[pl.ds(0, 9)], S_DX)
    for store in stores:
        store.wait()


def place(*refs):
    sems = refs[6]
    copies = [pltpu.make_async_copy(refs[i], refs[i + 3], sems.at[i]) for i in range(3)]
    for copy in copies:
        copy.start()
    for copy in copies:
        copy.wait()


def body(inputs, weights, cotangent):
    norm = 1.0 / math.sqrt(inputs.shape[0] * cotangent.shape[1] * 8 * inputs.shape[2])
    vmem = pl.BlockSpec(memory_space=pltpu.VMEM)
    hbm = pl.BlockSpec(memory_space=pl.ANY)
    out, dx, dw = pl.pallas_call(
        functools.partial(kernel, norm),
        out_shape=(
            pltpu.VMEM((8, 32, 128), BF16),
            pltpu.VMEM((2, 128, 128), BF16),
            pltpu.VMEM((3, 3, 32, 128), F32),
        ),
        in_specs=[hbm] * 3,
        out_specs=[hbm] * 3,
        scratch_shapes=[
            pltpu.VMEM((8, 32, 128), BF16),
            pltpu.VMEM((2, 128, 128), BF16),
            pltpu.VMEM((3, 3, 32, 128), F32),
            pltpu.VMEM((8, 32, 128), BF16),
            pltpu.VMEM((8, 2, 128, 128), BF16),
            pltpu.VMEM((4, 3, 3, 32, 128), BF16),
            pltpu.VMEM((2, 4, 9, 32, 128), BF16),
            pltpu.VMEM((2048, 384), BF16),
            pltpu.VMEM((2304, 384), BF16),
            pltpu.VMEM((128, 2304), BF16),
            pltpu.VMEM((384, 384), BF16),
            pltpu.VMEM((384, 384), BF16),
            pltpu.VMEM((10, 2, 128, 128), F32),
            pltpu.VMEM((2, 4, 2, 128, 128), F32),
            pltpu.VMEM((384, 384), F32),
            pltpu.VMEM((4, 3, 32, 384), F32),
            pltpu.VMEM((3, 3, 32, 384), F32),
            pltpu.VMEM((2, 4, PIECES, 9, 8, 128), F32),
            pltpu.VMEM((4, PIECES, 9, 8, 128), F32),
            pltpu.VMEM((3, PIECES, 9, 8, 128), F32),
            pltpu.VMEM((WAVES, 7, 16, 128), BF16),
            pltpu.VMEM((WAVES, 7, 16, 128), BF16),
            pltpu.VMEM((WAVES, 2, 8, 128), F32),
            pltpu.VMEM((WAVES, 2, 8, 128), F32),
            pltpu.SemaphoreType.DMA((N_SEND,)),
            pltpu.SemaphoreType.DMA((N_RECV,)),
            pltpu.SemaphoreType.DMA((3,)),
            pltpu.SemaphoreType.DMA((3,)),
        ],
        compiler_params=pltpu.CompilerParams(collective_id=0, has_side_effects=True),
        name="conv_layer",
    )(inputs[0], weights, cotangent[0])
    out, dx, dw = pl.pallas_call(
        place,
        out_shape=(
            jax.ShapeDtypeStruct((8, 32, 128), BF16),
            jax.ShapeDtypeStruct((2, 128, 128), BF16),
            jax.ShapeDtypeStruct((3, 3, 32, 128), F32),
        ),
        in_specs=[vmem] * 3,
        out_specs=[hbm] * 3,
        scratch_shapes=[pltpu.SemaphoreType.DMA((3,))],
        name="place_results",
    )(*(pltpu.with_memory_space_constraint(v, pltpu.VMEM) for v in (out, dx, dw)))
    return out[None], dx[None], dw


def solution(mesh):
    return jax.shard_map(
        body,
        mesh=mesh,
        in_specs=(
            P(None, "filt", None, "chan"),
            P(None, None, "filt", "chan"),
            P(None, "chan", "filt", None),
        ),
        out_specs=(
            P(None, "chan", "filt", None),
            P(None, "filt", None, "chan"),
            P(None, None, "filt", "chan"),
        ),
        check_vma=False,
    )
```
